768 devices in a mesh: dp: 96 (over y, z), tensor: 8 (over x, core).
Axes of the slice: x: 4, y: 8, z: 12, core: 2. Of those that a mesh axis runs over, the one named last changes fastest.
Arguments:
- gradients: bfloat16 [96, 1344, 4096], P('dp', None, 'tensor'), may hold values from -12 to 12
- error_buffer: bfloat16 [96, 1344, 4096], P('dp', None, 'tensor'), may hold values from -6 to 6
- warm_basis: float32 [4096, 32], P('tensor'), may hold values from -6 to 6
Outputs:
- new_errors: bfloat16 [96, 1344, 4096], P('dp', None, 'tensor')
- new_basis: float32 [4096, 32], P('tensor')
The draws below stay inside these ranges and needn't reach their ends.
All inputs are finite; a program needn't handle non-finite values.
Results may differ from the reference program's by a relative error of at most 0.001.
Values sent between devices are 32-bit elements; how exact they have to be, the bound alone decides.
A program may use at most 32 MiB of HBM per device.

```python
import jax
import jax.numpy as jnp
from jax import lax

ROWS = 16128
COLS = 4096
RANK = 32
REPLICAS = 8
SPLIT = 12


def block_levels(stream_key, dims, shards, least, high):
    loudness = 1.0
    for dim, parts in shards:
        draws = jax.random.uniform(jax.random.fold_in(jax.random.fold_in(stream_key, 6), dim), (parts,), jnp.float32, least / len(shards), high / len(shards))
        loudness = loudness * jnp.repeat(jnp.exp(draws), dims[dim] // parts).reshape((-1,) + (1,) * (len(dims) - 1 - dim))
    return loudness


def bell_draw(rng, dims, width, bound, pieces=(), dtype=jnp.bfloat16):
    values = width * jax.random.normal(rng, dims, jnp.float32)
    if pieces:
        values = values * block_levels(rng, dims, pieces, -0.22, 0.18)
    return jnp.clip(values, -bound, bound).astype(dtype)


def setup_inputs(seed: int = 0) -> dict:
    streams_of = jax.random.split(jax.random.key(seed), 4)
    return {
        "gradients": bell_draw(streams_of[0], (REPLICAS * SPLIT, ROWS // SPLIT, COLS), 2.0, 12.0, ((0, 96), (2, 8))),
        "error_buffer": bell_draw(streams_of[1], (REPLICAS * SPLIT, ROWS // SPLIT, COLS), 1.0, 6.0, ((0, 96), (2, 8))),
        "warm_basis": bell_draw(streams_of[2], (COLS, RANK), 1.0, 6.0, ((0, 8),), jnp.float32),
    }


def reference(gradients, error_buffer, warm_basis):
    highest = lax.Precision.HIGHEST
    grads = gradients.reshape(REPLICAS, ROWS, COLS)
    errors = error_buffer.reshape(REPLICAS, ROWS, COLS)

    def left_step(total, pair):
        grad_slab, error_slab = pair
        merged = grad_slab.astype(jnp.float32) + error_slab.astype(jnp.float32)
        return (total + jnp.dot(merged, warm_basis, precision=highest), None)
    left_sum, _ = lax.scan(left_step, jnp.zeros((ROWS, RANK), jnp.float32), (grads, errors))
    left_factor = left_sum / REPLICAS
    gram_matrix = jnp.dot(left_factor.T, left_factor, precision=highest)
    lower_factor = jnp.linalg.cholesky(gram_matrix)
    basis_left = lax.linalg.triangular_solve(lower_factor, left_factor, left_side=False, lower=True, transpose_a=True)

    def right_step(total, pair):
        grad_slab, error_slab = pair
        merged = grad_slab.astype(jnp.float32) + error_slab.astype(jnp.float32)
        return (total + jnp.dot(merged.T, basis_left, precision=highest), None)
    right_sum, _ = lax.scan(right_step, jnp.zeros((COLS, RANK), jnp.float32), (grads, errors))
    new_basis = right_sum / REPLICAS
    rebuilt = jnp.dot(basis_left, new_basis.T, precision=highest)

    def update(pair):
        grad_slab, error_slab = pair
        merged = grad_slab.astype(jnp.float32) + error_slab.astype(jnp.float32)
        return (merged - rebuilt).astype(jnp.bfloat16)
    new_errors = lax.map(update, (grads, errors))
    return (new_errors.reshape(REPLICAS * SPLIT, ROWS // SPLIT, COLS), new_basis)
```

```python
import jax
import jax.numpy as jnp
from jax import lax
from jax.experimental import pallas as pl
from jax.experimental.pallas import tpu as pltpu
from jax.sharding import PartitionSpec as P

MESH = pl.DeviceIdType.MESH
HIGHEST = lax.Precision.HIGHEST
F32 = jnp.float32
BF16 = jnp.bfloat16

NY = 8
NZ = 12
NT = 8
ROWS = 1344
COLS = 512
RANK = 32
GROUPS = 4
GROUP_ROWS = 384
HALF = 192
PIECE = GROUP_ROWS // NT
CHUNKS = 3
CHUNK = PIECE // CHUNKS
RCOLS = 256

ORDER8 = (4, 3, 5, 2, 6, 1, 7)
ORDER12 = (6, 5, 7, 4, 8, 3, 9, 2, 10, 1, 11)


def split2(x):
    hi = x.astype(BF16)
    return hi, (x - hi.astype(F32)).astype(BF16)


def split3(x):
    hi = x.astype(BF16)
    rest = x - hi.astype(F32)
    mid = rest.astype(BF16)
    return hi, mid, (rest - mid.astype(F32)).astype(BF16)


def row_bands(x, group):
    n = x.shape[1]
    parts = []
    if group:
        parts.append(jnp.zeros((RANK * group, n), x.dtype))
    parts.append(x)
    if group < GROUPS - 1:
        parts.append(jnp.zeros((RANK * (GROUPS - 1 - group), n), x.dtype))
    return jnp.concatenate(parts, axis=0)


def inverse_lower(gram):
    lane = lax.broadcasted_iota(jnp.int32, (RANK, 128), 1)
    row = lax.broadcasted_iota(jnp.int32, (RANK, 128), 0)
    a = jnp.where(lane < RANK, gram, jnp.where(lane == row + RANK, 1.0, 0.0))
    for k in range(RANK - 1):
        pivot = a[k : k + 1, :]
        factor = a[:, k : k + 1] * (1.0 / pivot[:, k : k + 1])
        factor = jnp.where(row[:, :1] > k, factor, 0.0)
        a = a - factor * pivot
    diagonal = jnp.sum(jnp.where(lane == row, a, 0.0), axis=1, keepdims=True)
    inv = a * lax.rsqrt(diagonal)
    inv = jnp.where((lane >= RANK) & (lane < 2 * RANK), inv, 0.0)
    inv = inv + pltpu.roll(inv, 2 * RANK, 1)
    return inv + pltpu.roll(inv, RANK, 1)


def comm_kernel(
    g_hbm, e_hbm, wt_ref, p_out, rt_out, l_out,
    gv, ev, part, xbuf, ybuf, pfull, rpart, rsbuf, zbuf, gbuf, rfull,
    load_sem, xs, xr, ys, yr, ps, pr, gs, gr, rs, rr, zs, zr, fs, fr,
):
    dp = lax.axis_index("dp")
    t = lax.axis_index("tensor")
    y = lax.div(dp, NZ)
    z = lax.rem(dp, NZ)

    def t_peer(k):
        return {"dp": dp, "tensor": lax.rem(t + k, NT)}

    def y_peer(k):
        return {"dp": lax.rem(y + k, NY) * NZ + z, "tensor": t}

    def z_peer(k):
        return {"dp": y * NZ + lax.rem(z + k, NZ), "tensor": t}

    def send(src, dst, ssem, rsem, peer):
        copy = pltpu.make_async_remote_copy(
            src_ref=src, dst_ref=dst, send_sem=ssem, recv_sem=rsem, device_id=peer, device_id_type=MESH
        )
        copy.start()
        return copy

    loads = []
    for j in range(GROUPS):
        rows = pl.ds(GROUP_ROWS * j, GROUP_ROWS if j < GROUPS - 1 else HALF)
        pair = [
            pltpu.make_async_copy(g_hbm.at[rows], gv.at[rows], load_sem.at[0, j]),
            pltpu.make_async_copy(e_hbm.at[rows], ev.at[rows], load_sem.at[1, j]),
        ]
        for copy in pair:
            copy.start()
        loads.append(pair)

    barrier = pltpu.get_barrier_semaphore()
    for k in ORDER12:
        pl.semaphore_signal(barrier, inc=1, device_id=z_peer(k), device_id_type=MESH)
    for k in ORDER8:
        pl.semaphore_signal(barrier, inc=1, device_id=y_peer(k), device_id_type=MESH)
        pl.semaphore_signal(barrier, inc=1, device_id=t_peer(k), device_id_type=MESH)

    w_hi, w_lo = split2(wt_ref[...] * (1.0 / NY))
    acc = [None, None]
    nt_dims = (((1,), (1,)), ((), ()))
    for j in range(GROUPS):
        weights = jnp.concatenate([row_bands(w_hi, j), row_bands(w_lo, j)], axis=0)
        for copy in loads[j]:
            copy.wait()
        for h in range(2 if j < GROUPS - 1 else 1):
            start = GROUP_ROWS * j + HALF * h
            for ref in (gv, ev):
                term = lax.dot_general(
                    ref[start : start + HALF, :], weights, nt_dims, preferred_element_type=F32
                )
                acc[h] = term if acc[h] is None else acc[h] + term
    for h in range(2):
        packed = acc[h][:, :128] + acc[h][:, 128:]
        for i in range(NT // 2):
            part[h * (NT // 2) + i] = packed[PIECE * i : PIECE * (i + 1)]

    pl.semaphore_wait(barrier, NZ + NY + NT - 3)

    sent = []
    got_x = {}
    for c in range(CHUNKS):
        rows = pl.ds(CHUNK * c, CHUNK)
        for k in ORDER8:
            copy = send(
                part.at[lax.rem(t + k, NT), rows], xbuf.at[k - 1, rows], xs.at[k - 1, c], xr.at[k - 1, c], t_peer(k)
            )
            sent.append(copy)
            got_x[k, c] = copy
    got_y = {}
    for c in range(CHUNKS):
        rows = pl.ds(CHUNK * c, CHUNK)
        total = part[t, rows]
        for k in reversed(ORDER8):
            got_x[k, c].wait_recv()
            total = total + xbuf[k - 1, rows]
        ybuf[y, rows] = total
        for k in ORDER8:
            copy = send(ybuf.at[y, rows], ybuf.at[y, rows], ys.at[k - 1, c], yr.at[k - 1, c], y_peer(k))
            sent.append(copy)
            got_y[k, c] = copy
    got_p = []
    for c in range(CHUNKS):
        rows = pl.ds(CHUNK * c, CHUNK)
        for k in reversed(ORDER8):
            got_y[k, c].wait_recv()
        total = ybuf[0, rows]
        for i in range(1, NY):
            total = total + ybuf[i, rows]
        pfull[t, rows] = total
        for k in ORDER8:
            copy = send(pfull.at[t, rows], pfull.at[t, rows], ps.at[k - 1, c], pr.at[k - 1, c], t_peer(k))
            sent.append(copy)
            got_p.append(copy)
    for copy in got_p:
        copy.wait_recv()

    left = jnp.concatenate([pfull[i] for i in range(NT)], axis=0)
    p_out[...] = left
    left_t = left.T

    blocks = jnp.dot(left_t, left, precision=HIGHEST, preferred_element_type=F32)
    lane8 = lax.broadcasted_iota(jnp.int32, (8, 128), 1)
    tile = jnp.zeros((8, 128), F32)
    for q in range(RANK // 8):
        rows8 = None
        for j in range(GROUPS):
            band = blocks[RANK * j + 8 * q : RANK * j + 8 * q + 8, :]
            band = jnp.where(lax.div(lane8, RANK) == j, band, 0.0)
            rows8 = band if rows8 is None else rows8 + band
        rows8 = rows8 + pltpu.roll(rows8, 64, 1)
        rows8 = rows8 + pltpu.roll(rows8, 32, 1)
        tile = jnp.where(lax.div(lane8, RANK) == q, rows8, tile)
    gbuf[z] = tile
    got_g = []
    for k in ORDER12:
        copy = send(gbuf.at[z], gbuf.at[z], gs.at[k - 1], gr.at[k - 1], z_peer(k))
        sent.append(copy)
        got_g.append(copy)

    bands = []
    for j in range(GROUPS):
        bands.append(left_t[RANK * j : RANK * (j + 1), : GROUP_ROWS if j < GROUPS - 1 else HALF])
    lt = jnp.concatenate(bands, axis=1)
    lhs = jnp.concatenate(split3(lt * (1.0 / NY)), axis=0)
    right = jnp.dot(lhs, gv[...], preferred_element_type=F32) + jnp.dot(
        lhs, ev[...], preferred_element_type=F32
    )
    right = right[:RANK] + (right[RANK : 2 * RANK] + right[2 * RANK :])
    for i in range(NY):
        q, h = i // 2, i % 2
        rpart[i] = right[8 * q : 8 * q + 8, RCOLS * h : RCOLS * (h + 1)]
    got_r = {}
    for k in ORDER8:
        copy = send(rpart.at[lax.rem(y + k, NY)], rsbuf.at[k - 1], rs.at[k - 1], rr.at[k - 1], y_peer(k))
        sent.append(copy)
        got_r[k] = copy
    total = rpart[y]
    for k in reversed(ORDER8):
        got_r[k].wait_recv()
        total = total + rsbuf[k - 1]
    zbuf[z] = total
    got_z = []
    for k in ORDER12:
        copy = send(zbuf.at[z], zbuf.at[z], zs.at[k - 1], zr.at[k - 1], z_peer(k))
        sent.append(copy)
        got_z.append(copy)

    for copy in got_g:
        copy.wait_recv()
    tile = gbuf[0]
    for i in range(1, NZ):
        tile = tile + gbuf[i]
    rows = [tile] + [pltpu.roll(tile, 128 - 32 * q, 1) for q in range(1, RANK // 8)]
    l_out[...] = inverse_lower(jnp.concatenate(rows, axis=0))

    for copy in got_z:
        copy.wait_recv()
    total = zbuf[0]
    for i in range(1, NZ):
        total = total + zbuf[i]
    rfull[y] = total
    got_f = []
    for k in ORDER8:
        copy = send(rfull.at[y], rfull.at[y], fs.at[k - 1], fr.at[k - 1], y_peer(k))
        sent.append(copy)
        got_f.append(copy)
    for copy in got_f:
        copy.wait_recv()
    for i in range(NY):
        q, h = i // 2, i % 2
        rt_out[8 * q : 8 * q + 8, RCOLS * h : RCOLS * (h + 1)] = rfull[i]
    for copy in sent:
        copy.wait_send()


def update_kernel(g_hbm, e_hbm, p_ref, rt_ref, l_ref, err_hbm, nb_ref, gv, ev, ov, load_sem, out_sem):
    blocks = ROWS // HALF
    loads = []
    for b in range(blocks):
        rows = pl.ds(HALF * b, HALF)
        pair = [
            pltpu.make_async_copy(g_hbm.at[rows], gv.at[rows], load_sem.at[0, b]),
            pltpu.make_async_copy(e_hbm.at[rows], ev.at[rows], load_sem.at[1, b]),
        ]
        for copy in pair:
            copy.start()
        loads.append(pair)
    inv = l_ref[...]
    basis_t = jnp.dot(inv[:, :RANK], rt_ref[...], precision=HIGHEST, preferred_element_type=F32)
    nb_ref[...] = basis_t
    lane = lax.broadcasted_iota(jnp.int32, (RANK, 128), 1)
    diag = jnp.concatenate(
        [jnp.where(lax.div(lane, RANK) == j, inv, 0.0) for j in range(GROUPS)], axis=0
    )
    left_basis = lax.dot_general(
        p_ref[...], diag, (((1,), (1,)), ((), ())), precision=HIGHEST, preferred_element_type=F32
    )
    b_hi, b_lo = split2(left_basis)
    lhs = jnp.concatenate([b_hi, b_lo], axis=1)
    n_hi, n_lo = split2(basis_t)
    stores = []
    for b in range(blocks):
        j, h = b // 2, b % 2
        hi = row_bands(n_hi, j)
        rebuilt = jnp.dot(
            lhs[HALF * h : HALF * (h + 1)], jnp.concatenate([hi, hi], axis=0), preferred_element_type=F32
        ) + jnp.dot(b_hi[HALF * h : HALF * (h + 1)], row_bands(n_lo, j), preferred_element_type=F32)
        for copy in loads[b]:
            copy.wait()
        sl = slice(HALF * b, HALF * (b + 1))
        merged = gv[sl, :].astype(F32) + ev[sl, :].astype(F32)
        ov[sl, :] = (merged - rebuilt).astype(BF16)
        rows = pl.ds(HALF * b, HALF)
        copy = pltpu.make_async_copy(ov.at[rows], err_hbm.at[rows], out_sem.at[b])
        copy.start()
        stores.append(copy)
    for copy in stores:
        copy.wait()


def on_device(gradients, error_buffer, warm_basis):
    g, e = gradients[0], error_buffer[0]
    vmem = pl.BlockSpec(memory_space=pltpu.VMEM)
    anyspace = pl.BlockSpec(memory_space=pl.ANY)
    dma = pltpu.SemaphoreType.DMA
    left, right_t, inv = pl.pallas_call(
        comm_kernel,
        name="factors",
        out_shape=(
            jax.ShapeDtypeStruct((GROUP_ROWS, 128), F32),
            jax.ShapeDtypeStruct((RANK, COLS), F32),
            jax.ShapeDtypeStruct((RANK, 128), F32),
        ),
        in_specs=[anyspace, anyspace, vmem],
        out_specs=(vmem, vmem, vmem),
        scratch_shapes=[
            pltpu.VMEM((ROWS, COLS), BF16),
            pltpu.VMEM((ROWS, COLS), BF16),
            pltpu.VMEM((NT, PIECE, 128), F32),
            pltpu.VMEM((NT - 1, PIECE, 128), F32),
            pltpu.VMEM((NY, PIECE, 128), F32),
            pltpu.VMEM((NT, PIECE, 128), F32),
            pltpu.VMEM((NY, 8, RCOLS), F32),
            pltpu.VMEM((NY - 1, 8, RCOLS), F32),
            pltpu.VMEM((NZ, 8, RCOLS), F32),
            pltpu.VMEM((NZ, 8, 128), F32),
            pltpu.VMEM((NY, 8, RCOLS), F32),
            dma((2, GROUPS)),
            dma((NT - 1, CHUNKS)), dma((NT - 1, CHUNKS)),
            dma((NY - 1, CHUNKS)), dma((NY - 1, CHUNKS)),
            dma((NT - 1, CHUNKS)), dma((NT - 1, CHUNKS)),
            dma((NZ - 1,)), dma((NZ - 1,)),
            dma((NY - 1,)), dma((NY - 1,)),
            dma((NZ - 1,)), dma((NZ - 1,)),
            dma((NY - 1,)), dma((NY - 1,)),
        ],
        compiler_params=pltpu.CompilerParams(collective_id=0, has_side_effects=True),
    )(g, e, warm_basis.T)
    new_errors, basis_t = pl.pallas_call(
        update_kernel,
        name="update",
        out_shape=(
            jax.ShapeDtypeStruct((ROWS, COLS), BF16),
            jax.ShapeDtypeStruct((RANK, COLS), F32),
        ),
        in_specs=[anyspace, anyspace, vmem, vmem, vmem],
        out_specs=(anyspace, vmem),
        scratch_shapes=[
            pltpu.VMEM((ROWS, COLS), BF16),
            pltpu.VMEM((ROWS, COLS), BF16),
            pltpu.VMEM((ROWS, COLS), BF16),
            dma((2, ROWS // HALF)),
            dma((ROWS // HALF,)),
        ],
    )(g, e, left, right_t, inv)
    return new_errors[None], basis_t.T


def solution(mesh):
    placed = (P("dp", None, "tensor"), P("dp", None, "tensor"), P("tensor", None))
    return jax.shard_map(
        on_device,
        mesh=mesh,
        in_specs=placed,
        out_specs=(P("dp", None, "tensor"), P("tensor", None)),
        check_vma=False,
    )
```

```python
import jax
import jax.numpy as jnp
from jax import lax
from jax.experimental import pallas as pl
from jax.experimental.pallas import tpu as pltpu
from jax.sharding import PartitionSpec as P

MESH = pl.DeviceIdType.MESH
HIGHEST = lax.Precision.HIGHEST
F32 = jnp.float32
BF16 = jnp.bfloat16

NY = 8
NZ = 12
NT = 8
ROWS = 1344
COLS = 512
RANK = 32
GROUPS = 4
GROUP_ROWS = 384
HALF = 192
PIECE = GROUP_ROWS // NT
CHUNKS = 3
CHUNK = PIECE // CHUNKS
RCHUNKS = 2

ORDER8 = (4, 3, 5, 2, 6, 1, 7)
ORDER12 = (6, 5, 7, 4, 8, 3, 9, 2, 10, 1, 11)


def split2(x):
    hi = x.astype(BF16)
    return hi, (x - hi.astype(F32)).astype(BF16)


def split3(x):
    hi = x.astype(BF16)
    rest = x - hi.astype(F32)
    mid = rest.astype(BF16)
    return hi, mid, (rest - mid.astype(F32)).astype(BF16)


def row_bands(x, group):
    n = x.shape[1]
    parts = []
    if group:
        parts.append(jnp.zeros((RANK * group, n), x.dtype))
    parts.append(x)
    if group < GROUPS - 1:
        parts.append(jnp.zeros((RANK * (GROUPS - 1 - group), n), x.dtype))
    return jnp.concatenate(parts, axis=0)


def inverse_lower(gram):
    lane = lax.broadcasted_iota(jnp.int32, (RANK, 128), 1)
    row = lax.broadcasted_iota(jnp.int32, (RANK, 128), 0)
    a = jnp.where(lane < RANK, gram, jnp.where(lane == row + RANK, 1.0, 0.0))
    for k in range(RANK - 1):
        pivot = a[k : k + 1, :]
        factor = a[:, k : k + 1] * (1.0 / pivot[:, k : k + 1])
        factor = jnp.where(row[:, :1] > k, factor, 0.0)
        a = a - factor * pivot
    diagonal = jnp.sum(jnp.where(lane == row, a, 0.0), axis=1, keepdims=True)
    inv = a * lax.rsqrt(diagonal)
    inv = jnp.where((lane >= RANK) & (lane < 2 * RANK), inv, 0.0)
    inv = inv + pltpu.roll(inv, 2 * RANK, 1)
    return inv + pltpu.roll(inv, RANK, 1)


def factors_kernel(
    g_hbm, e_hbm, wt_hbm, gv, ev, lhs_ref, nb_ref,
    wt, part, xbuf, ybuf, pfull, rpart, rsbuf, zbuf, gbuf, rfull,
    load_sem, send_sem, xr, yr, pr, gr, rr, zr, fr,
):
    dp = lax.axis_index("dp")
    t = lax.axis_index("tensor")
    y = lax.div(dp, NZ)
    z = lax.rem(dp, NZ)

    def t_peer(k):
        return {"dp": dp, "tensor": lax.rem(t + k, NT)}

    def y_peer(k):
        return {"dp": lax.rem(y + k, NY) * NZ + z, "tensor": t}

    def z_peer(k):
        return {"dp": y * NZ + lax.rem(z + k, NZ), "tensor": t}

    def send(src, dst, ssem, rsem, peer):
        copy = pltpu.make_async_remote_copy(
            src_ref=src, dst_ref=dst, send_sem=ssem, recv_sem=rsem, device_id=peer, device_id_type=MESH
        )
        copy.start()

    def arrived(ref, sem):
        pltpu.make_async_remote_copy(
            src_ref=ref, dst_ref=ref, send_sem=send_sem.at[0], recv_sem=sem, device_id=t_peer(1), device_id_type=MESH
        ).wait_recv()

    def left_here(ref, sem):
        pltpu.make_async_remote_copy(
            src_ref=ref, dst_ref=ref, send_sem=sem, recv_sem=xr.at[0], device_id=t_peer(1), device_id_type=MESH
        ).wait_send()

    barrier = pltpu.get_barrier_semaphore()
    for k in ORDER8:
        pl.semaphore_signal(barrier, inc=1, device_id=y_peer(k), device_id_type=MESH)
    wt_load = pltpu.make_async_copy(wt_hbm, wt, load_sem.at[2 * GROUPS])
    wt_load.start()
    loads = []
    for j in range(GROUPS):
        rows = pl.ds(GROUP_ROWS * j, GROUP_ROWS if j < GROUPS - 1 else HALF)
        pair = [
            pltpu.make_async_copy(g_hbm.at[rows], gv.at[rows], load_sem.at[2 * j]),
            pltpu.make_async_copy(e_hbm.at[rows], ev.at[rows], load_sem.at[2 * j + 1]),
        ]
        for copy in pair:
            copy.start()
        loads.append(pair)
    for k in ORDER12:
        pl.semaphore_signal(barrier, inc=1, device_id=z_peer(k), device_id_type=MESH)
    for k in ORDER8:
        pl.semaphore_signal(barrier, inc=1, device_id=t_peer(k), device_id_type=MESH)

    wt_load.wait()
    w_hi, w_lo = split2(wt[...] * (1.0 / NY))
    acc = [None, None]
    nt_dims = (((1,), (1,)), ((), ()))
    for j in range(GROUPS):
        weights = jnp.concatenate([row_bands(w_hi, j), row_bands(w_lo, j)], axis=0)
        for copy in loads[j]:
            copy.wait()
        for h in range(2 if j < GROUPS - 1 else 1):
            start = GROUP_ROWS * j + HALF * h
            for ref in (gv, ev):
                term = lax.dot_general(
                    ref[start : start + HALF, :], weights, nt_dims, preferred_element_type=F32
                )
                acc[h] = term if acc[h] is None else acc[h] + term
    for h in range(2):
        packed = acc[h][:, :128] + acc[h][:, 128:]
        for i in range(NT // 2):
            part[h * (NT // 2) + i] = packed[PIECE * i : PIECE * (i + 1)]

    pl.semaphore_wait(barrier, NZ + NY + NT - 3)

    for c in range(CHUNKS):
        rows = pl.ds(CHUNK * c, CHUNK)
        for k in ORDER8:
            send(part.at[lax.rem(t + k, NT), rows], xbuf.at[k - 1, rows], send_sem.at[0], xr.at[c], t_peer(k))
    for c in range(CHUNKS):
        rows = pl.ds(CHUNK * c, CHUNK)
        arrived(xbuf.at[:, rows], xr.at[c])
        total = part[t, rows]
        for i in range(NT - 1):
            total = total + xbuf[i, rows]
        ybuf[y, rows] = total
        for k in ORDER8:
            send(ybuf.at[y, rows], ybuf.at[y, rows], send_sem.at[1], yr.at[c], y_peer(k))
    for c in range(CHUNKS):
        rows = pl.ds(CHUNK * c, CHUNK)
        arrived(ybuf.at[pl.ds(0, NY - 1), rows], yr.at[c])
        total = ybuf[0, rows]
        for i in range(1, NY):
            total = total + ybuf[i, rows]
        pfull[t, rows] = total
        for k in ORDER8:
            send(pfull.at[t, rows], pfull.at[t, rows], send_sem.at[2], pr, t_peer(k))
    arrived(pfull.at[pl.ds(0, NT - 1)], pr)

    left = jnp.concatenate([pfull[i] for i in range(NT)], axis=0)
    left_t = left.T

    bands = []
    for j in range(GROUPS):
        bands.append(left_t[RANK * j : RANK * (j + 1), : GROUP_ROWS if j < GROUPS - 1 else HALF])
    lt = jnp.concatenate(bands, axis=1)
    lhs = jnp.concatenate(split3(lt * (1.0 / NY)), axis=0)
    right = jnp.dot(lhs, gv[...], preferred_element_type=F32) + jnp.dot(
        lhs, ev[...], preferred_element_type=F32
    )
    right = right[:RANK] + (right[RANK : 2 * RANK] + right[2 * RANK :])
    for c in range(RCHUNKS):
        for i in range(NY):
            q, h = i // 2, 2 * (i % 2) + c
            rpart[c, i] = right[8 * q : 8 * q + 8, 128 * h : 128 * (h + 1)]
    for c in range(RCHUNKS):
        for k in ORDER8:
            send(rpart.at[c, lax.rem(y + k, NY)], rsbuf.at[c, k - 1], send_sem.at[3], rr.at[c], y_peer(k))

    blocks = jnp.dot(left_t, left, precision=HIGHEST, preferred_element_type=F32)
    lane8 = lax.broadcasted_iota(jnp.int32, (8, 128), 1)
    tile = jnp.zeros((8, 128), F32)
    for q in range(RANK // 8):
        rows8 = None
        for j in range(GROUPS):
            band = blocks[RANK * j + 8 * q : RANK * j + 8 * q + 8, :]
            band = jnp.where(lax.div(lane8, RANK) == j, band, 0.0)
            rows8 = band if rows8 is None else rows8 + band
        rows8 = rows8 + pltpu.roll(rows8, 64, 1)
        rows8 = rows8 + pltpu.roll(rows8, 32, 1)
        tile = jnp.where(lax.div(lane8, RANK) == q, rows8, tile)
    gbuf[z] = tile
    for k in ORDER12:
        send(gbuf.at[z], gbuf.at[z], send_sem.at[4], gr, z_peer(k))

    for c in range(RCHUNKS):
        arrived(rsbuf.at[c], rr.at[c])
        total = rpart[c, y]
        for i in range(NY - 1):
            total = total + rsbuf[c, i]
        zbuf[c, z] = total
        for k in ORDER12:
            send(zbuf.at[c, z], zbuf.at[c, z], send_sem.at[5], zr.at[c], z_peer(k))

    arrived(gbuf.at[pl.ds(0, NZ - 1)], gr)
    tile = gbuf[0]
    for i in range(1, NZ):
        tile = tile + gbuf[i]
    rows = [tile] + [pltpu.roll(tile, 128 - 32 * q, 1) for q in range(1, RANK // 8)]
    inv = inverse_lower(jnp.concatenate(rows, axis=0))

    for c in range(RCHUNKS):
        arrived(zbuf.at[c, pl.ds(0, NZ - 1)], zr.at[c])
        total = zbuf[c, 0]
        for i in range(1, NZ):
            total = total + zbuf[c, i]
        rfull[c, y] = total
        for k in ORDER8:
            send(rfull.at[c, y], rfull.at[c, y], send_sem.at[6], fr, y_peer(k))

    lane = lax.broadcasted_iota(jnp.int32, (RANK, 128), 1)
    diag = jnp.concatenate(
        [jnp.where(lax.div(lane, RANK) == j, inv, 0.0) for j in range(GROUPS)], axis=0
    )
    left_basis = lax.dot_general(left, diag, nt_dims, precision=HIGHEST, preferred_element_type=F32)
    b_hi = left_basis.astype(BF16).astype(F32)
    b_lo = left_basis - b_hi
    wide = lax.broadcasted_iota(jnp.int32, (GROUP_ROWS, 128), 1)
    for j in range(GROUPS):
        n = GROUP_ROWS if j < GROUPS - 1 else HALF
        first = pltpu.roll(b_hi[:n], (128 - RANK * j) % 128, 1) if j else b_hi[:n]
        second = pltpu.roll(b_lo[:n], (128 + RANK - RANK * j) % 128, 1) if j != 1 else b_lo[:n]
        third = pltpu.roll(b_hi[:n], (128 + 2 * RANK - RANK * j) % 128, 1) if j != 2 else b_hi[:n]
        mixed = jnp.where(wide[:n] < RANK, first, jnp.where(wide[:n] < 2 * RANK, second, third))
        mixed = jnp.where(wide[:n] < 3 * RANK, mixed, 0.0)
        lhs_ref[GROUP_ROWS * j : GROUP_ROWS * j + n] = mixed.astype(BF16)
    i_hi, i_mid, i_lo = split3(inv[:, :RANK])
    inv_lhs = jnp.concatenate([i_hi, i_hi, i_mid, i_hi, i_mid, i_lo], axis=1)

    arrived(rfull.at[:, pl.ds(0, NY - 1)], fr)

    rt = jnp.concatenate(
        [jnp.concatenate([rfull[h % 2, 2 * q + h // 2] for h in range(4)], axis=1) for q in range(RANK // 8)],
        axis=0,
    )
    r_hi, r_mid, r_lo = split3(rt)
    basis_t = jnp.dot(
        inv_lhs, jnp.concatenate([r_hi, r_mid, r_hi, r_lo, r_mid, r_hi], axis=0), preferred_element_type=F32
    )
    nb_ref[...] = basis_t
    left_here(xbuf, send_sem.at[0])
    left_here(xbuf, send_sem.at[1])
    left_here(xbuf, send_sem.at[2])
    left_here(rsbuf, send_sem.at[3])
    left_here(gbuf.at[pl.ds(0, NZ - 1)], send_sem.at[4])
    left_here(zbuf.at[:, pl.ds(0, NZ - 1)], send_sem.at[5])
    left_here(rsbuf, send_sem.at[6])


def update_kernel(gv, ev, lhs_ref, basis_ref, err_hbm, nb_hbm, out, sem):
    blocks = ROWS // HALF
    stores = [pltpu.make_async_copy(basis_ref, nb_hbm, sem.at[blocks])]
    stores[0].start()
    n_hi, n_lo = split2(basis_ref[...])
    rhs = jnp.concatenate([n_hi, n_hi, n_lo, jnp.zeros_like(n_lo)], axis=0)
    for b in range(blocks):
        sl = slice(HALF * b, HALF * (b + 1))
        rebuilt = jnp.dot(lhs_ref[sl, :], rhs, preferred_element_type=F32)
        merged = gv[sl, :].astype(F32) + ev[sl, :].astype(F32)
        out[sl, :] = (merged - rebuilt).astype(BF16)
        rows = pl.ds(HALF * b, HALF)
        copy = pltpu.make_async_copy(out.at[rows], err_hbm.at[rows], sem.at[b])
        copy.start()
        stores.append(copy)
    for copy in stores:
        copy.wait()


def on_device(gradients, error_buffer, warm_basis):
    vmem = pl.BlockSpec(memory_space=pltpu.VMEM)
    anyspace = pl.BlockSpec(memory_space=pl.ANY)
    dma = pltpu.SemaphoreType.DMA
    wide = (ROWS, COLS)
    kept = pl.pallas_call(
        factors_kernel,
        name="factors",
        out_shape=(
            pltpu.VMEM(wide, BF16),
            pltpu.VMEM(wide, BF16),
            pltpu.VMEM((ROWS, 128), BF16),
            pltpu.VMEM((RANK, COLS), F32),
        ),
        in_specs=[anyspace, anyspace, anyspace],
        out_specs=(vmem, vmem, vmem, vmem),
        scratch_shapes=[
            pltpu.VMEM((RANK, COLS), F32),
            pltpu.VMEM((NT, PIECE, 128), F32),
            pltpu.VMEM((NT - 1, PIECE, 128), F32),
            pltpu.VMEM((NY, PIECE, 128), F32),
            pltpu.VMEM((NT, PIECE, 128), F32),
            pltpu.VMEM((RCHUNKS, NY, 8, 128), F32),
            pltpu.VMEM((RCHUNKS, NY - 1, 8, 128), F32),
            pltpu.VMEM((RCHUNKS, NZ, 8, 128), F32),
            pltpu.VMEM((NZ, 8, 128), F32),
            pltpu.VMEM((RCHUNKS, NY, 8, 128), F32),
            dma((2 * GROUPS + 1,)),
            dma((7,)),
            dma((CHUNKS,)), dma((CHUNKS,)), dma,
            dma, dma((RCHUNKS,)), dma((RCHUNKS,)), dma,
        ],
        compiler_params=pltpu.CompilerParams(
            collective_id=0, has_side_effects=True, vmem_limit_bytes=24 * 1024 * 1024
        ),
    )(*(pltpu.with_memory_space_constraint(x, pltpu.HBM) for x in (gradients[0], error_buffer[0], warm_basis.T)))
    new_errors, basis_t = pl.pallas_call(
        update_kernel,
        name="update",
        out_shape=(jax.ShapeDtypeStruct(wide, BF16), jax.ShapeDtypeStruct((RANK, COLS), F32)),
        in_specs=[vmem, vmem, vmem, vmem],
        out_specs=(anyspace, anyspace),
        scratch_shapes=[pltpu.VMEM(wide, BF16), dma((ROWS // HALF + 1,))],
        compiler_params=pltpu.CompilerParams(vmem_limit_bytes=24 * 1024 * 1024),
    )(*(pltpu.with_memory_space_constraint(x, pltpu.VMEM) for x in kept))
    return new_errors[None], basis_t.T


def solution(mesh):
    placed = (P("dp", None, "tensor"), P("dp", None, "tensor"), P("tensor", None))
    return jax.shard_map(
        on_device,
        mesh=mesh,
        in_specs=placed,
        out_specs=(P("dp", None, "tensor"), P("tensor", None)),
        check_vma=False,
    )
```

```python
import functools

import jax
import jax.numpy as jnp
from jax import lax
from jax.experimental import pallas as pl
from jax.experimental.pallas import tpu as pltpu
from jax.sharding import PartitionSpec as P

MESH = pl.DeviceIdType.MESH
HIGHEST = lax.Precision.HIGHEST
F32 = jnp.float32
BF16 = jnp.bfloat16

NY = 8
NZ = 12
NX = 4
ROWS = 1344
COLS = 512
RANK = 32
GROUPS = 4
GROUP_ROWS = 384
HALF = 192
CHUNKS = 3
PIECE = 128 // NX
RCHUNKS = 2

ORDER4 = (2, 1, 3)
ORDER8 = (4, 3, 5, 2, 6, 1, 7)
ORDER12 = (1, 11, 2, 10, 3, 9, 4, 8, 5, 7, 6)


def chunk_rows(c):
    rows = []
    for j in range(GROUPS):
        length = min(128, (GROUP_ROWS if j < GROUPS - 1 else HALF) - 128 * c)
        if length > 0:
            rows.append((j, GROUP_ROWS * j + 128 * c, length))
    return rows


def split2(x):
    hi = x.astype(BF16)
    return hi, (x - hi.astype(F32)).astype(BF16)


def split3(x):
    hi = x.astype(BF16)
    rest = x - hi.astype(F32)
    mid = rest.astype(BF16)
    return hi, mid, (rest - mid.astype(F32)).astype(BF16)


def row_bands(x, group):
    n = x.shape[1]
    parts = []
    if group:
        parts.append(jnp.zeros((RANK * group, n), x.dtype))
    parts.append(x)
    if group < GROUPS - 1:
        parts.append(jnp.zeros((RANK * (GROUPS - 1 - group), n), x.dtype))
    return jnp.concatenate(parts, axis=0)


def inverse_lower(gram):
    lane = lax.broadcasted_iota(jnp.int32, (RANK, 128), 1)
    row = lax.broadcasted_iota(jnp.int32, (RANK, 128), 0)
    a = jnp.where(lane < RANK, gram, jnp.where(lane == row + RANK, 1.0, 0.0))
    for k in range(RANK - 1):
        pivot = a[k : k + 1, :]
        factor = a[:, k : k + 1] * (1.0 / pivot[:, k : k + 1])
        factor = jnp.where(row[:, :1] > k, factor, 0.0)
        a = a - factor * pivot
    diagonal = jnp.sum(jnp.where(lane == row, a, 0.0), axis=1, keepdims=True)
    inv = a * lax.rsqrt(diagonal)
    inv = jnp.where((lane >= RANK) & (lane < 2 * RANK), inv, 0.0)
    inv = inv + pltpu.roll(inv, 2 * RANK, 1)
    return inv + pltpu.roll(inv, RANK, 1)


def factors_kernel(
    g_hbm, e_hbm, wt_hbm, gv, ev, lhs_ref, nb_ref,
    wt, part, xbuf, ybuf, pfull, rpart, rbuf0, rbuf1, zbuf, zsum, gbuf, gsum, rfull,
    load_sem, send_sem, xr, yr, pr, gr, gm, rr0, rr1, zr, fr, reach,
):
    dp = lax.axis_index("dp")
    t = lax.axis_index("tensor")
    y = lax.div(dp, NZ)
    z = lax.rem(dp, NZ)
    x = lax.div(t, 2)
    core = lax.rem(t, 2)

    def x_peer(k, c):
        return {"dp": dp, "tensor": lax.rem(x + k, NX) * 2 + c}

    def y_peer(k, c):
        return {"dp": lax.rem(y + k, NY) * NZ + z, "tensor": x * 2 + c}

    def z_peer(k):
        return {"dp": y * NZ + lax.rem(z + k, NZ), "tensor": t}

    def send(src, dst, ssem, rsem, peer):
        pltpu.make_async_remote_copy(
            src_ref=src, dst_ref=dst, send_sem=ssem, recv_sem=rsem, device_id=peer, device_id_type=MESH
        ).start()

    def arrived(ref, sem):
        pltpu.make_async_remote_copy(
            src_ref=ref, dst_ref=ref, send_sem=send_sem.at[0], recv_sem=sem, device_id=x_peer(1, core), device_id_type=MESH
        ).wait_recv()

    def left_here(ref, sem):
        pltpu.make_async_remote_copy(
            src_ref=ref, dst_ref=ref, send_sem=sem, recv_sem=xr.at[0], device_id=x_peer(1, core), device_id_type=MESH
        ).wait_send()

    def signal(sem, peer):
        pl.semaphore_signal(sem, inc=1, device_id=peer, device_id_type=MESH)

    on_core0 = functools.partial(pl.when, core == 0)
    on_core1 = functools.partial(pl.when, core == 1)

    wt_load = pltpu.make_async_copy(wt_hbm, wt, load_sem.at[2 * GROUPS])
    wt_load.start()
    loads = []
    for j in range(GROUPS):
        rows = pl.ds(GROUP_ROWS * j, GROUP_ROWS if j < GROUPS - 1 else HALF)
        loads.append(pltpu.make_async_copy(g_hbm.at[rows], gv.at[rows], load_sem.at[2 * j]))
        loads.append(pltpu.make_async_copy(e_hbm.at[rows], ev.at[rows], load_sem.at[2 * j + 1]))
        loads[-2].start()
        loads[-1].start()

    barrier = pltpu.get_barrier_semaphore()

    @on_core1()
    def _():
        for k in ORDER8:
            signal(barrier, y_peer(k, 1))
            signal(barrier, y_peer(k, 0))
        for k in (1, NZ - 1):
            signal(barrier, z_peer(k))
        for k in ORDER4:
            signal(barrier, x_peer(k, 1))
            signal(barrier, x_peer(k, 0))
        signal(barrier, x_peer(0, 0))

    @on_core0()
    def _():
        for k in ORDER8:
            signal(barrier, y_peer(k, 1))
        for k in ORDER4 + (0,):
            signal(barrier, x_peer(k, 1))

    wt_load.wait()
    w_hi, w_lo = split2(wt[...] * (1.0 / NY))
    weights = [jnp.concatenate([row_bands(w_hi, j), row_bands(w_lo, j)], axis=0) for j in range(GROUPS)]
    nt_dims = (((1,), (1,)), ((), ()))
    for c in range(CHUNKS):
        acc = None
        for j, start, length in chunk_rows(c):
            if c == 0:
                loads[2 * j].wait()
                loads[2 * j + 1].wait()
            for ref in (gv, ev):
                term = lax.dot_general(
                    ref[start : start + length, :], weights[j], nt_dims, preferred_element_type=F32
                )
                if acc is None:
                    acc = term
                elif length == 128:
                    acc = acc + term
                else:
                    acc = jnp.concatenate([acc[:length] + term, acc[length:]], axis=0)
        packed = acc[:, :128] + acc[:, 128:]
        for i in range(NX):
            part[c, i] = packed[PIECE * i : PIECE * (i + 1)]
        if c == 0:

            @on_core1()
            def _():
                pl.semaphore_wait(barrier, 2 * (NX - 1) + 1 + 2 * (NY - 1) + 2)
                for k in (1, NZ - 1):
                    signal(reach.at[0], z_peer(k))

            @on_core0()
            def _():
                pl.semaphore_wait(barrier, NX + NY - 1)

        @on_core1()
        def _():
            for k in ORDER4:
                send(part.at[c, lax.rem(x + k, NX)], xbuf.at[c, k - 1], send_sem.at[0], xr.at[c], x_peer(k, 1))

        @on_core0()
        def _():
            for k in ORDER4 + (0,):
                send(part.at[c, lax.rem(x + k, NX)], xbuf.at[c, NX - 1 + k], send_sem.at[0], xr.at[c], x_peer(k, 1))

    @on_core1()
    def _():
        for c in range(CHUNKS):
            arrived(xbuf.at[c], xr.at[c])
            total = part[c, x]
            for i in range(2 * NX - 1):
                total = total + xbuf[c, i]
            ybuf[c, y] = total
            for k in ORDER8:
                send(ybuf.at[c, y], ybuf.at[c, y], send_sem.at[1], yr.at[c], y_peer(k, 1))
        pl.semaphore_wait(reach.at[0], 2)
        for k in (2, NZ - 2):
            signal(reach.at[1], z_peer(k))
        for c in range(CHUNKS):
            if c == 1:
                pl.semaphore_wait(reach.at[1], 2)
                for k in (2, NZ - 2):
                    signal(reach.at[2], z_peer(k))
            arrived(ybuf.at[c, pl.ds(0, NY - 1)], yr.at[c])
            total = ybuf[c, 0]
            for i in range(1, NY):
                total = total + ybuf[c, i]
            pfull[c, x] = total
            for k in ORDER4:
                send(pfull.at[c, x], pfull.at[c, x], send_sem.at[2], pr.at[c], x_peer(k, 0))
                send(pfull.at[c, x], pfull.at[c, x], send_sem.at[2], pr.at[c], x_peer(k, 1))
            send(pfull.at[c, x], pfull.at[c, x], send_sem.at[2], pr.at[c], x_peer(0, 0))

    right = None
    for c in range(CHUNKS):

        @on_core1()
        def _():
            arrived(pfull.at[c, pl.ds(0, NX - 1)], pr.at[c])

        @on_core0()
        def _():
            arrived(pfull.at[c], pr.at[c])

        left_t = jnp.concatenate([pfull[c, i] for i in range(NX)], axis=0).T
        rows = chunk_rows(c)
        lt = jnp.concatenate([left_t[RANK * j : RANK * (j + 1), :length] for j, _, length in rows], axis=1)
        lhs = jnp.concatenate(split3(lt * (1.0 / NY)), axis=0)
        for ref in (gv, ev):
            block = jnp.concatenate([ref[start : start + length, :] for _, start, length in rows], axis=0)
            term = jnp.dot(lhs, block, preferred_element_type=F32)
            right = term if right is None else right + term
    right = right[:RANK] + (right[RANK : 2 * RANK] + right[2 * RANK :])
    for c in range(RCHUNKS):
        for i in range(NY):
            q, h = i // 2, 2 * (i % 2) + c
            rpart[c, i] = right[8 * q : 8 * q + 8, 128 * h : 128 * (h + 1)]
    left = jnp.concatenate([pfull[c, i] for c in range(CHUNKS) for i in range(NX)], axis=0)

    @on_core0()
    def _():
        for c in range(RCHUNKS):
            for k in ORDER8 + (0,):
                send(rpart.at[c, lax.rem(y + k, NY)], rbuf0.at[c, k], send_sem.at[3], rr0.at[c], y_peer(k, 1))
        arrived(gsum, gm)

    @on_core1()
    def _():
        for c in range(RCHUNKS):
            for k in ORDER8:
                send(rpart.at[c, lax.rem(y + k, NY)], rbuf1.at[c, k - 1], send_sem.at[3], rr1.at[c], y_peer(k, 1))

        blocks = jnp.dot(left.T, left, precision=HIGHEST, preferred_element_type=F32)
        lane8 = lax.broadcasted_iota(jnp.int32, (8, 128), 1)
        tile = jnp.zeros((8, 128), F32)
        for q in range(RANK // 8):
            rows8 = None
            for j in range(GROUPS):
                band = blocks[RANK * j + 8 * q : RANK * j + 8 * q + 8, :]
                band = jnp.where(lax.div(lane8, RANK) == j, band, 0.0)
                rows8 = band if rows8 is None else rows8 + band
            rows8 = rows8 + pltpu.roll(rows8, 64, 1)
            rows8 = rows8 + pltpu.roll(rows8, 32, 1)
            tile = jnp.where(lax.div(lane8, RANK) == q, rows8, tile)
        gbuf[z] = tile
        pl.semaphore_wait(reach.at[2], 2)
        for k in ORDER12:
            send(gbuf.at[z], gbuf.at[z], send_sem.at[4], gr, z_peer(k))

        for c in range(RCHUNKS):
            arrived(rbuf1.at[c], rr1.at[c])
            total = rpart[c, y]
            for i in range(NY - 1):
                total = total + rbuf1[c, i]
            zbuf[c, z, 1] = total
            arrived(rbuf0.at[c], rr0.at[c])
            total = rbuf0[c, 0]
            for i in range(1, NY):
                total = total + rbuf0[c, i]
            zbuf[c, z, 0] = total
            for k in ORDER12:
                send(zbuf.at[c, z], zbuf.at[c, z], send_sem.at[5], zr.at[c], z_peer(k))

        arrived(gbuf.at[pl.ds(0, NZ - 1)], gr)
        tile = gbuf[0]
        for i in range(1, NZ):
            tile = tile + gbuf[i]
        gsum[...] = tile
        send(gsum, gsum, send_sem.at[6], gm, x_peer(0, 0))

    tile = gsum[...]
    rows = [tile] + [pltpu.roll(tile, 128 - 32 * q, 1) for q in range(1, RANK // 8)]
    inv = inverse_lower(jnp.concatenate(rows, axis=0))

    @on_core1()
    def _():
        for c in range(RCHUNKS):
            arrived(zbuf.at[c, pl.ds(0, NZ - 1)], zr.at[c])
            total = zbuf[c, 0]
            for i in range(1, NZ):
                total = total + zbuf[c, i]
            zsum[c] = total[0]
            rfull[c, y] = total[1]
            for k in ORDER8:
                send(zsum.at[c], rfull.at[c, y], send_sem.at[7], fr, y_peer(k, 0))
                send(rfull.at[c, y], rfull.at[c, y], send_sem.at[8], fr, y_peer(k, 1))
            send(zsum.at[c], rfull.at[c, y], send_sem.at[7], fr, x_peer(0, 0))

    lane = lax.broadcasted_iota(jnp.int32, (RANK, 128), 1)
    diag = jnp.concatenate(
        [jnp.where(lax.div(lane, RANK) == j, inv, 0.0) for j in range(GROUPS)], axis=0
    )
    left_basis = lax.dot_general(left, diag, nt_dims, precision=HIGHEST, preferred_element_type=F32)
    b_hi = left_basis.astype(BF16).astype(F32)
    b_lo = left_basis - b_hi
    wide = lax.broadcasted_iota(jnp.int32, (GROUP_ROWS, 128), 1)
    for j in range(GROUPS):
        n = GROUP_ROWS if j < GROUPS - 1 else HALF
        first = pltpu.roll(b_hi[:n], (128 - RANK * j) % 128, 1) if j else b_hi[:n]
        second = pltpu.roll(b_lo[:n], (128 + RANK - RANK * j) % 128, 1) if j != 1 else b_lo[:n]
        third = pltpu.roll(b_hi[:n], (128 + 2 * RANK - RANK * j) % 128, 1) if j != 2 else b_hi[:n]
        mixed = jnp.where(wide[:n] < RANK, first, jnp.where(wide[:n] < 2 * RANK, second, third))
        mixed = jnp.where(wide[:n] < 3 * RANK, mixed, 0.0)
        lhs_ref[GROUP_ROWS * j : GROUP_ROWS * j + n] = mixed.astype(BF16)
    i_hi, i_mid, i_lo = split3(inv[:, :RANK])
    inv_lhs = jnp.concatenate([i_hi, i_hi, i_mid, i_hi, i_mid, i_lo], axis=1)

    @on_core1()
    def _():
        arrived(rfull.at[:, pl.ds(0, NY - 1)], fr)

    @on_core0()
    def _():
        arrived(rfull, fr)

    rt = jnp.concatenate(
        [jnp.concatenate([rfull[h % 2, 2 * q + h // 2] for h in range(4)], axis=1) for q in range(RANK // 8)],
        axis=0,
    )
    r_hi, r_mid, r_lo = split3(rt)
    basis_t = jnp.dot(
        inv_lhs, jnp.concatenate([r_hi, r_mid, r_hi, r_lo, r_mid, r_hi], axis=0), preferred_element_type=F32
    )
    nb_ref[...] = basis_t

    @on_core0()
    def _():
        left_here(part, send_sem.at[0])
        left_here(rpart, send_sem.at[3])

    @on_core1()
    def _():
        left_here(part.at[:, pl.ds(0, NX - 1)], send_sem.at[0])
        left_here(xbuf, send_sem.at[1])
        left_here(xbuf, send_sem.at[2])
        left_here(rbuf1, send_sem.at[3])
        left_here(gbuf.at[pl.ds(0, NZ - 1)], send_sem.at[4])
        left_here(zbuf.at[:, pl.ds(0, NZ - 1)], send_sem.at[5])
        left_here(gsum, send_sem.at[6])
        left_here(rbuf0, send_sem.at[7])
        left_here(rbuf1, send_sem.at[8])


def update_kernel(gv, ev, lhs_ref, basis_ref, err_hbm, nb_hbm, out, sem):
    blocks = ROWS // HALF
    stores = [pltpu.make_async_copy(basis_ref, nb_hbm, sem.at[blocks])]
    stores[0].start()
    n_hi, n_lo = split2(basis_ref[...])
    rhs = jnp.concatenate([n_hi, n_hi, n_lo, jnp.zeros_like(n_lo)], axis=0)
    for b in range(blocks):
        sl = slice(HALF * b, HALF * (b + 1))
        rebuilt = jnp.dot(lhs_ref[sl, :], rhs, preferred_element_type=F32)
        merged = gv[sl, :].astype(F32) + ev[sl, :].astype(F32)
        out[sl, :] = (merged - rebuilt).astype(BF16)
        rows = pl.ds(HALF * b, HALF)
        copy = pltpu.make_async_copy(out.at[rows], err_hbm.at[rows], sem.at[b])
        copy.start()
        stores.append(copy)
    for copy in stores:
        copy.wait()


def on_device(gradients, error_buffer, warm_basis):
    vmem = pl.BlockSpec(memory_space=pltpu.VMEM)
    anyspace = pl.BlockSpec(memory_space=pl.ANY)
    dma = pltpu.SemaphoreType.DMA
    wide = (ROWS, COLS)
    kept = pl.pallas_call(
        factors_kernel,
        name="factors",
        out_shape=(
            pltpu.VMEM(wide, BF16),
            pltpu.VMEM(wide, BF16),
            pltpu.VMEM((ROWS, 128), BF16),
            pltpu.VMEM((RANK, COLS), F32),
        ),
        in_specs=[anyspace, anyspace, anyspace],
        out_specs=(vmem, vmem, vmem, vmem),
        scratch_shapes=[
            pltpu.VMEM((RANK, COLS), F32),
            pltpu.VMEM((CHUNKS, NX, PIECE, 128), F32),
            pltpu.VMEM((CHUNKS, 2 * NX - 1, PIECE, 128), F32),
            pltpu.VMEM((CHUNKS, NY, PIECE, 128), F32),
            pltpu.VMEM((CHUNKS, NX, PIECE, 128), F32),
            pltpu.VMEM((RCHUNKS, NY, 8, 128), F32),
            pltpu.VMEM((RCHUNKS, NY, 8, 128), F32),
            pltpu.VMEM((RCHUNKS, NY - 1, 8, 128), F32),
            pltpu.VMEM((RCHUNKS, NZ, 2, 8, 128), F32),
            pltpu.VMEM((RCHUNKS, 8, 128), F32),
            pltpu.VMEM((NZ, 8, 128), F32),
            pltpu.VMEM((8, 128), F32),
            pltpu.VMEM((RCHUNKS, NY, 8, 128), F32),
            dma((2 * GROUPS + 1,)),
            dma((9,)),
            dma((CHUNKS,)), dma((CHUNKS,)), dma((CHUNKS,)),
            dma, dma, dma((RCHUNKS,)), dma((RCHUNKS,)), dma((RCHUNKS,)), dma,
            pltpu.SemaphoreType.REGULAR((3,)),
        ],
        compiler_params=pltpu.CompilerParams(
            collective_id=0, has_side_effects=True, vmem_limit_bytes=24 * 1024 * 1024
        ),
    )(*(pltpu.with_memory_space_constraint(x, pltpu.HBM) for x in (gradients[0], error_buffer[0], warm_basis.T)))
    new_errors, basis_t = pl.pallas_call(
        update_kernel,
        name="update",
        out_shape=(jax.ShapeDtypeStruct(wide, BF16), jax.ShapeDtypeStruct((RANK, COLS), F32)),
        in_specs=[vmem, vmem, vmem, vmem],
        out_specs=(anyspace, anyspace),
        scratch_shapes=[pltpu.VMEM(wide, BF16), dma((ROWS // HALF + 1,))],
        compiler_params=pltpu.CompilerParams(vmem_limit_bytes=24 * 1024 * 1024),
    )(*(pltpu.with_memory_space_constraint(x, pltpu.VMEM) for x in kept))
    return new_errors[None], basis_t.T


def solution(mesh):
    placed = (P("dp", None, "tensor"), P("dp", None, "tensor"), P("tensor", None))
    return jax.shard_map(
        on_device,
        mesh=mesh,
        in_specs=placed,
        out_specs=(P("dp", None, "tensor"), P("tensor", None)),
        check_vma=False,
    )
```

```python
import functools

import jax
import jax.numpy as jnp
from jax import lax
from jax.experimental import pallas as pl
from jax.experimental.pallas import tpu as pltpu
from jax.sharding import PartitionSpec as P

MESH = pl.DeviceIdType.MESH
HIGHEST = lax.Precision.HIGHEST
F32 = jnp.float32
BF16 = jnp.bfloat16

NY = 8
NZ = 12
NX = 4
ROWS = 1344
COLS = 512
RANK = 32
GROUPS = 4
GROUP_ROWS = ROWS // GROUPS
BLOCK = 192
CHUNKS = ((0, 64, 64), (64, 96, 96), (160, 128, 128), (288, 48, 64))
PACKED = sum(padded for _, _, padded in CHUNKS)
RCHUNKS = 2

FIRST = 3
ORDER4 = (2, 1, 3)
ORDER8 = (4, 3, 5, 2, 6, 1, 7)


def pad_rows(block, rows):
    if block.shape[0] == rows:
        return block
    return jnp.concatenate([block, jnp.zeros((rows - block.shape[0], block.shape[1]), block.dtype)], axis=0)


def split2(x):
    hi = x.astype(BF16)
    return hi, (x - hi.astype(F32)).astype(BF16)


def split3(x):
    hi = x.astype(BF16)
    rest = x - hi.astype(F32)
    mid = rest.astype(BF16)
    return hi, mid, (rest - mid.astype(F32)).astype(BF16)


def inverse_lower(gram):
    lane = lax.broadcasted_iota(jnp.int32, (RANK, 128), 1)
    row = lax.broadcasted_iota(jnp.int32, (RANK, 128), 0)
    a = jnp.where(lane < RANK, gram, jnp.where(lane == row + RANK, 1.0, 0.0))
    for k in range(RANK - 1):
        pivot = a[k : k + 1, :]
        factor = a[:, k : k + 1] * (1.0 / pivot[:, k : k + 1])
        factor = jnp.where(row[:, :1] > k, factor, 0.0)
        a = a - factor * pivot
    diagonal = jnp.sum(jnp.where(lane == row, a, 0.0), axis=1, keepdims=True)
    inv = a * lax.rsqrt(diagonal)
    inv = jnp.where((lane >= RANK) & (lane < 2 * RANK), inv, 0.0)
    inv = inv + pltpu.roll(inv, 2 * RANK, 1)
    return inv + pltpu.roll(inv, RANK, 1)


def factors_kernel(
    g_hbm, e_hbm, wt_hbm, merged, lhs_ref, nb_ref,
    gv, ev, wt, wall, part, xbuf, ybuf, pfull, rpart, rbuf0, rbuf1, zbuf, zsum, gbuf, gsum, rfull, sizes,
    load_sem, send_sem, xr, yr, pr, gr, gm, rr0, rr1, zr, fr, reach_y, reach_z,
):
    dp = lax.axis_index("dp")
    t = lax.axis_index("tensor")
    y = lax.div(dp, NZ)
    z = lax.rem(dp, NZ)
    x = lax.div(t, 2)
    core = lax.rem(t, 2)

    def x_peer(k, c):
        return {"dp": dp, "tensor": lax.rem(x + k, NX) * 2 + c}

    def y_peer(k, c):
        return {"dp": lax.rem(y + k, NY) * NZ + z, "tensor": x * 2 + c}

    def z_peer(k):
        return {"dp": y * NZ + lax.rem(z + k, NZ), "tensor": t}

    z_peers = [{"dp": y * NZ + i + lax.div(i + NZ - z, NZ), "tensor": t} for i in range(NZ - 1)]

    def send(src, dst, ssem, rsem, peer):
        pltpu.make_async_remote_copy(
            src_ref=src, dst_ref=dst, send_sem=ssem, recv_sem=rsem, device_id=peer, device_id_type=MESH
        ).start()

    def arrived(ref, sem):
        pltpu.make_async_remote_copy(
            src_ref=ref, dst_ref=ref, send_sem=send_sem.at[0], recv_sem=sem, device_id=x_peer(1, core), device_id_type=MESH
        ).wait_recv()

    def left_here(ref, sem):
        pltpu.make_async_remote_copy(
            src_ref=ref, dst_ref=ref, send_sem=sem, recv_sem=xr.at[0], device_id=x_peer(1, core), device_id_type=MESH
        ).wait_send()

    def signal(sem, peer):
        pl.semaphore_signal(sem, inc=1, device_id=peer, device_id_type=MESH)

    on_core0 = functools.partial(pl.when, core == 0)
    on_core1 = functools.partial(pl.when, core == 1)

    wt_load = pltpu.make_async_copy(wt_hbm, wt, load_sem.at[2 * len(CHUNKS)])
    wt_load.start()

    def load(c):
        rows = pl.ds(*CHUNKS[c][:2])
        return [
            pltpu.make_async_copy(hbm.at[:, rows], ref.at[:, rows], load_sem.at[2 * c + i])
            for i, (hbm, ref) in enumerate(((g_hbm, gv), (e_hbm, ev)))
        ]

    loads = [load(c) for c in range(len(CHUNKS))]
    for copy in loads[0]:
        copy.start()

    barrier = pltpu.get_barrier_semaphore()

    @on_core1()
    def _():
        for k in ORDER4:
            signal(barrier, x_peer(k, 1))
            signal(barrier, x_peer(k, 0))
        for k in (1, NY - 1):
            signal(barrier, y_peer(k, 1))
        for k in (1, NZ - 1):
            signal(barrier, z_peer(k))
        signal(barrier, x_peer(0, 0))

    @on_core0()
    def _():
        for k in ORDER4 + (0,):
            signal(barrier, x_peer(k, 1))

    for copy in loads[1]:
        copy.start()

    wt_load.wait()
    for copy in loads[2] + loads[3]:
        copy.start()
    w_wide = jnp.concatenate([wt[...] * (1.0 / NY)] * GROUPS, axis=0).T
    group = lax.div(lax.broadcasted_iota(jnp.int32, (COLS, 128), 1), RANK)
    for j in range(GROUPS):
        banded = jnp.where(group == j, w_wide, 0.0)
        wall[COLS * j : COLS * (j + 1), :] = jnp.concatenate(split2(banded), axis=1)
    for c, (first, length, padded) in enumerate(CHUNKS):
        for copy in loads[c]:
            copy.wait()
        halves = [
            pad_rows(jnp.concatenate([ref[j, first : first + length, :] for j in range(GROUPS)], axis=1), padded)
            for ref in (gv, ev)
        ]
        acc = jnp.dot(jnp.concatenate(halves, axis=0), wall[...], preferred_element_type=F32)
        acc = acc[:padded] + acc[padded:]
        packed = acc[:, :128] + acc[:, 128:]
        piece = padded // NX
        for i in range(NX):
            part[c, i, :piece] = packed[piece * i : piece * (i + 1)]
        rows = pl.ds(0, piece)
        if c == 0:

            @on_core1()
            def _():
                pl.semaphore_wait(barrier, 2 * (NX - 1) + 1 + 2 + 2)
                for k in (1, NY - 1):
                    signal(reach_y.at[0], y_peer(k, 1))
                for k in (1, NZ - 1):
                    signal(reach_z.at[0], z_peer(k))

            @on_core0()
            def _():
                pl.semaphore_wait(barrier, NX)

        @on_core1()
        def _():
            for k in ORDER4:
                send(part.at[c, lax.rem(x + k, NX), rows], xbuf.at[c, k - 1, rows], send_sem.at[0], xr.at[c], x_peer(k, 1))

        @on_core0()
        def _():
            for k in ORDER4 + (0,):
                send(part.at[c, lax.rem(x + k, NX), rows], xbuf.at[c, NX - 1 + k, rows], send_sem.at[0], xr.at[c], x_peer(k, 1))

    @on_core1()
    def _():
        pl.semaphore_wait(reach_y.at[0], 2)
        for k in (2, NY - 2):
            signal(reach_y.at[1], y_peer(k, 1))
        for c, (_, _, padded) in enumerate(CHUNKS):
            rows = pl.ds(0, padded // NX)
            arrived(xbuf.at[c, :, rows], xr.at[c])
            if c == 0:
                pl.semaphore_wait(reach_y.at[1], 2)
            total = part[c, x, rows]
            for i in range(2 * NX - 1):
                total = total + xbuf[c, i, rows]
            ybuf[c, y, rows] = total
            for k in ORDER8:
                send(ybuf.at[c, y, rows], ybuf.at[c, y, rows], send_sem.at[1], yr.at[c], y_peer(k, 1))
        pl.semaphore_wait(reach_z.at[0], 2)
        for k in (2, NZ - 2):
            signal(reach_z.at[1], z_peer(k))
        for c, (_, _, padded) in enumerate(CHUNKS):
            if c == 1:
                pl.semaphore_wait(reach_z.at[1], 2)
                for k in (2, NZ - 2):
                    signal(reach_z.at[2], z_peer(k))
            rows = pl.ds(0, padded // NX)
            arrived(ybuf.at[c, pl.ds(0, NY - 1), rows], yr.at[c])
            total = ybuf[c, 0, rows]
            for i in range(1, NY):
                total = total + ybuf[c, i, rows]
            pfull[c, x, rows] = total
            for k in ORDER4:
                send(pfull.at[c, x, rows], pfull.at[c, x, rows], send_sem.at[2], pr.at[c], x_peer(k, 0))
                send(pfull.at[c, x, rows], pfull.at[c, x, rows], send_sem.at[2], pr.at[c], x_peer(k, 1))
            send(pfull.at[c, x, rows], pfull.at[c, x, rows], send_sem.at[2], pr.at[c], x_peer(0, 0))

    right = None
    bands = []
    for c, (first, length, padded) in enumerate(CHUNKS):
        rows = pl.ds(0, padded // NX)

        @on_core1()
        def _():
            arrived(pfull.at[c, pl.ds(0, NX - 1), rows], pr.at[c])

        @on_core0()
        def _():
            arrived(pfull.at[c, :, rows], pr.at[c])

        bands.append(jnp.concatenate([pfull[c, i, rows] for i in range(NX)], axis=0)[:length])
        left_t = pad_rows(bands[-1], 128).T
        lt = [left_t[RANK * j : RANK * (j + 1)] for j in range(GROUPS)]
        depth = 128
        if length <= 64:
            depth = 64
            lt = [lt[j] + pltpu.roll(lt[j + 1], 64, 1) for j in range(0, GROUPS, 2)]
        lt = jnp.concatenate(lt, axis=1)
        lhs = jnp.concatenate(split3(lt * (1.0 / NY)), axis=0)
        for ref in (gv, ev):
            block = jnp.concatenate(
                [pad_rows(ref[j, first : first + length, :], depth) for j in range(GROUPS)], axis=0
            )
            term = jnp.dot(lhs, block, preferred_element_type=F32)
            right = term if right is None else right + term
    right = right[:RANK] + (right[RANK : 2 * RANK] + right[2 * RANK :])
    for c in range(RCHUNKS):
        for i in range(NY):
            q, h = i // 2, 2 * (i % 2) + c
            rpart[c, i] = right[8 * q : 8 * q + 8, 128 * h : 128 * (h + 1)]
    left = jnp.concatenate(bands, axis=0)

    @on_core0()
    def _():
        for c in range(RCHUNKS):
            for k in ORDER8 + (0,):
                send(rpart.at[c, lax.rem(y + k, NY)], rbuf0.at[c, k], send_sem.at[3], rr0.at[c], y_peer(k, 1))
        arrived(gsum, gm)

    @on_core1()
    def _():
        for c in range(RCHUNKS):
            for k in ORDER8:
                send(rpart.at[c, lax.rem(y + k, NY)], rbuf1.at[c, k - 1], send_sem.at[3], rr1.at[c], y_peer(k, 1))

        blocks = jnp.dot(left.T, left, precision=HIGHEST, preferred_element_type=F32)
        lane8 = lax.broadcasted_iota(jnp.int32, (8, 128), 1)
        tile = jnp.zeros((8, 128), F32)
        for q in range(RANK // 8):
            rows8 = None
            for j in range(GROUPS):
                band = blocks[RANK * j + 8 * q : RANK * j + 8 * q + 8, :]
                band = jnp.where(lax.div(lane8, RANK) == j, band, 0.0)
                rows8 = band if rows8 is None else rows8 + band
            rows8 = rows8 + pltpu.roll(rows8, 64, 1)
            rows8 = rows8 + pltpu.roll(rows8, 32, 1)
            tile = jnp.where(lax.div(lane8, RANK) == q, rows8, tile)
        gbuf[z] = tile
        pl.semaphore_wait(reach_z.at[2], 2)
        for peer in z_peers:
            send(gbuf.at[z], gbuf.at[z], send_sem.at[4], gr, peer)

        for c in range(RCHUNKS):
            arrived(rbuf1.at[c], rr1.at[c])
            total = rpart[c, y]
            for i in range(NY - 1):
                total = total + rbuf1[c, i]
            zbuf[c, z, 1] = total
            arrived(rbuf0.at[c], rr0.at[c])
            total = rbuf0[c, 0]
            for i in range(1, NY):
                total = total + rbuf0[c, i]
            zbuf[c, z, 0] = total
            for peer in z_peers[:FIRST]:
                send(zbuf.at[c, z], zbuf.at[c, z], send_sem.at[5], zr.at[c], peer)
        for peer in z_peers[FIRST:]:
            for c in range(RCHUNKS):
                send(zbuf.at[c, z], zbuf.at[c, z], send_sem.at[5], zr.at[c], peer)

        arrived(gbuf.at[pl.ds(0, NZ - 1)], gr)
        tile = gbuf[0]
        for i in range(1, NZ):
            tile = tile + gbuf[i]
        gsum[...] = tile
        send(gsum, gsum, send_sem.at[6], gm, x_peer(0, 0))

    tile = gsum[...]
    rows = [tile] + [pltpu.roll(tile, 128 - 32 * q, 1) for q in range(1, RANK // 8)]
    inv = inverse_lower(jnp.concatenate(rows, axis=0))

    @on_core1()
    def _():
        for c in range(RCHUNKS):
            arrived(zbuf.at[c, pl.ds(0, NZ - 1)], zr.at[c])
            total = zbuf[c, 0]
            for i in range(1, NZ):
                total = total + zbuf[c, i]
            zsum[c] = total[0]
            rfull[c, y] = total[1]
            for k in ORDER8:
                send(zsum.at[c], rfull.at[c, y], send_sem.at[7], fr, y_peer(k, 0))
                send(rfull.at[c, y], rfull.at[c, y], send_sem.at[8], fr, y_peer(k, 1))
            send(zsum.at[c], rfull.at[c, y], send_sem.at[7], fr, x_peer(0, 0))

    lane = lax.broadcasted_iota(jnp.int32, (RANK, 128), 1)
    diag = jnp.concatenate(
        [jnp.where(lax.div(lane, RANK) == j, inv, 0.0) for j in range(GROUPS)], axis=0
    )
    left_basis = lax.dot_general(left, diag, (((1,), (1,)), ((), ())), precision=HIGHEST, preferred_element_type=F32)
    b_hi = left_basis.astype(BF16).astype(F32)
    b_lo = left_basis - b_hi
    wide = lax.broadcasted_iota(jnp.int32, (GROUP_ROWS, 128), 1)
    for j in range(GROUPS):
        first = pltpu.roll(b_hi, (128 - RANK * j) % 128, 1) if j else b_hi
        second = pltpu.roll(b_lo, (128 + RANK - RANK * j) % 128, 1) if j != 1 else b_lo
        third = pltpu.roll(b_hi, (128 + 2 * RANK - RANK * j) % 128, 1) if j != 2 else b_hi
        mixed = jnp.where(wide < RANK, first, jnp.where(wide < 2 * RANK, second, third))
        mixed = jnp.where(wide < 3 * RANK, mixed, 0.0)
        lhs_ref[GROUP_ROWS * j : GROUP_ROWS * (j + 1)] = mixed.astype(BF16)
        merged[GROUP_ROWS * j : GROUP_ROWS * (j + 1)] = gv[j].astype(F32) + ev[j].astype(F32)
    i_hi, i_mid, i_lo = split3(inv[:, :RANK])
    inv_lhs = jnp.concatenate([i_hi, i_hi, i_mid, i_hi, i_mid, i_lo], axis=1)

    @on_core1()
    def _():
        arrived(rfull.at[:, pl.ds(0, NY - 1)], fr)

    @on_core0()
    def _():
        arrived(rfull, fr)

    rt = jnp.concatenate(
        [jnp.concatenate([rfull[h % 2, 2 * q + h // 2] for h in range(4)], axis=1) for q in range(RANK // 8)],
        axis=0,
    )
    r_hi, r_mid, r_lo = split3(rt)
    basis_t = jnp.dot(
        inv_lhs, jnp.concatenate([r_hi, r_mid, r_hi, r_lo, r_mid, r_hi], axis=0), preferred_element_type=F32
    )
    nb_ref[...] = basis_t

    packed_piece = pl.ds(0, PACKED // NX)

    @on_core0()
    def _():
        left_here(sizes.at[pl.ds(0, NX), packed_piece], send_sem.at[0])
        left_here(rpart, send_sem.at[3])

    @on_core1()
    def _():
        left_here(sizes.at[pl.ds(0, NX - 1), packed_piece], send_sem.at[0])
        left_here(sizes.at[pl.ds(0, NY - 1), packed_piece], send_sem.at[1])
        left_here(sizes.at[pl.ds(0, 2 * NX - 1), packed_piece], send_sem.at[2])
        left_here(rbuf1, send_sem.at[3])
        left_here(gbuf.at[pl.ds(0, NZ - 1)], send_sem.at[4])
        left_here(zbuf.at[:, pl.ds(0, NZ - 1)], send_sem.at[5])
        left_here(gsum, send_sem.at[6])
        left_here(rbuf0, send_sem.at[7])
        left_here(rbuf1, send_sem.at[8])


def update_kernel(merged, lhs_ref, basis_ref, err_hbm, nb_hbm, out, sem):
    blocks = ROWS // BLOCK
    stores = [pltpu.make_async_copy(basis_ref, nb_hbm, sem.at[blocks])]
    stores[0].start()
    n_hi, n_lo = split2(basis_ref[...])
    rhs = jnp.concatenate([n_hi, n_hi, n_lo, jnp.zeros_like(n_lo)], axis=0)
    for b in range(blocks):
        sl = slice(BLOCK * b, BLOCK * (b + 1))
        rebuilt = jnp.dot(lhs_ref[sl, :], rhs, preferred_element_type=F32)
        out[sl, :] = (merged[sl, :] - rebuilt).astype(BF16)
        rows = pl.ds(BLOCK * b, BLOCK)
        copy = pltpu.make_async_copy(out.at[rows], err_hbm.at[rows], sem.at[b])
        copy.start()
        stores.append(copy)
    for copy in stores:
        copy.wait()


def on_device(gradients, error_buffer, warm_basis):
    vmem = pl.BlockSpec(memory_space=pltpu.VMEM)
    anyspace = pl.BlockSpec(memory_space=pl.ANY)
    dma = pltpu.SemaphoreType.DMA
    wide = (ROWS, COLS)
    grouped = (GROUPS, GROUP_ROWS, COLS)
    nc, piece = len(CHUNKS), max(padded for _, _, padded in CHUNKS) // NX
    inputs = (gradients.reshape(grouped), error_buffer.reshape(grouped), warm_basis.T)
    kept = pl.pallas_call(
        factors_kernel,
        name="factors",
        out_shape=(
            pltpu.VMEM(wide, F32),
            pltpu.VMEM((ROWS, 128), BF16),
            pltpu.VMEM((RANK, COLS), F32),
        ),
        in_specs=[anyspace, anyspace, anyspace],
        out_specs=(vmem, vmem, vmem),
        scratch_shapes=[
            pltpu.VMEM(grouped, BF16),
            pltpu.VMEM(grouped, BF16),
            pltpu.VMEM((RANK, COLS), F32),
            pltpu.VMEM((GROUPS * COLS, 256), BF16),
            pltpu.VMEM((nc, NX, piece, 128), F32),
            pltpu.VMEM((nc, 2 * NX - 1, piece, 128), F32),
            pltpu.VMEM((nc, NY, piece, 128), F32),
            pltpu.VMEM((nc, NX, piece, 128), F32),
            pltpu.VMEM((RCHUNKS, NY, 8, 128), F32),
            pltpu.VMEM((RCHUNKS, NY, 8, 128), F32),
            pltpu.VMEM((RCHUNKS, NY - 1, 8, 128), F32),
            pltpu.VMEM((RCHUNKS, NZ, 2, 8, 128), F32),
            pltpu.VMEM((RCHUNKS, 8, 128), F32),
            pltpu.VMEM((NZ, 8, 128), F32),
            pltpu.VMEM((8, 128), F32),
            pltpu.VMEM((RCHUNKS, NY, 8, 128), F32),
            pltpu.VMEM((NY, PACKED // NX, 128), F32),
            dma((2 * nc + 1,)),
            dma((9,)),
            dma((nc,)), dma((nc,)), dma((nc,)),
            dma, dma, dma((RCHUNKS,)), dma((RCHUNKS,)), dma((RCHUNKS,)), dma,
            pltpu.SemaphoreType.REGULAR((2,)), pltpu.SemaphoreType.REGULAR((3,)),
        ],
        compiler_params=pltpu.CompilerParams(
            collective_id=0, has_side_effects=True, vmem_limit_bytes=24 * 1024 * 1024
        ),
    )(*(pltpu.with_memory_space_constraint(x, pltpu.HBM) for x in inputs))
    new_errors, basis_t = pl.pallas_call(
        update_kernel,
        name="update",
        out_shape=(jax.ShapeDtypeStruct(wide, BF16), jax.ShapeDtypeStruct((RANK, COLS), F32)),
        in_specs=[vmem, vmem, vmem],
        out_specs=(anyspace, anyspace),
        scratch_shapes=[pltpu.VMEM(wide, BF16), dma((ROWS // BLOCK + 1,))],
        compiler_params=pltpu.CompilerParams(vmem_limit_bytes=24 * 1024 * 1024),
    )(*(pltpu.with_memory_space_constraint(x, pltpu.VMEM) for x in kept))
    return new_errors[None], basis_t.T


def solution(mesh):
    placed = (P("dp", None, "tensor"), P("dp", None, "tensor"), P("tensor", None))
    return jax.shard_map(
        on_device,
        mesh=mesh,
        in_specs=placed,
        out_specs=(P("dp", None, "tensor"), P("tensor", None)),
        check_vma=False,
    )
```

```python
import functools

import jax
import jax.numpy as jnp
from jax import lax
from jax.experimental import pallas as pl
from jax.experimental.pallas import tpu as pltpu
from jax.sharding import PartitionSpec as P

MESH = pl.DeviceIdType.MESH
HIGHEST = lax.Precision.HIGHEST
F32 = jnp.float32
BF16 = jnp.bfloat16

NY = 8
NZ = 12
NX = 4
ROWS = 1344
COLS = 512
RANK = 32
GROUPS = 4
GROUP_ROWS = ROWS // GROUPS
BLOCK = 192
CHUNKS = ((0, 64, 64), (64, 96, 96), (160, 128, 128), (288, 48, 64))
PACKED = sum(padded for _, _, padded in CHUNKS)
RCHUNKS = 2

SENT0 = NX * PACKED // NX // 8 + RCHUNKS * NY
SENT1 = (17 * PACKED // NX // 8) + RCHUNKS * 7 + 11 + RCHUNKS * 11 * 2 + 1 + RCHUNKS * 15
FIRST = 1
ORDER4 = (2, 1, 3)
ORDER8 = (4, 3, 5, 2, 6, 1, 7)


def pad_rows(block, rows):
    if block.shape[0] == rows:
        return block
    return jnp.concatenate([block, jnp.zeros((rows - block.shape[0], block.shape[1]), block.dtype)], axis=0)


def split2(x):
    hi = x.astype(BF16)
    return hi, (x - hi.astype(F32)).astype(BF16)


def split3(x):
    hi = x.astype(BF16)
    rest = x - hi.astype(F32)
    mid = rest.astype(BF16)
    return hi, mid, (rest - mid.astype(F32)).astype(BF16)


def inverse_lower(gram):
    lane = lax.broadcasted_iota(jnp.int32, (RANK, 128), 1)
    row = lax.broadcasted_iota(jnp.int32, (RANK, 128), 0)
    a = jnp.where(lane < RANK, gram, jnp.where(lane == row + RANK, 1.0, 0.0))
    for k in range(RANK - 1):
        pivot = a[k : k + 1, :]
        factor = a[:, k : k + 1] * (1.0 / pivot[:, k : k + 1])
        factor = jnp.where(row[:, :1] > k, factor, 0.0)
        a = a - factor * pivot
    diagonal = jnp.sum(jnp.where(lane == row, a, 0.0), axis=1, keepdims=True)
    inv = a * lax.rsqrt(diagonal)
    inv = jnp.where((lane >= RANK) & (lane < 2 * RANK), inv, 0.0)
    inv = inv + pltpu.roll(inv, 2 * RANK, 1)
    return inv + pltpu.roll(inv, RANK, 1)


def factors_kernel(
    g_hbm, e_hbm, wt_hbm, merged, lhs_ref, nb_ref,
    both, wt, wall, part, xbuf, ybuf, pfull, rpart, rbuf, zbuf, zsum, gbuf, gsum, rfull, sizes,
    load_sem, send_sem, xr, yr, pr, gr, gm, rr, zr, fr, reach_y, reach_z,
):
    dp = lax.axis_index("dp")
    t = lax.axis_index("tensor")
    y = lax.div(dp, NZ)
    z = lax.rem(dp, NZ)
    x = lax.div(t, 2)
    core = lax.rem(t, 2)

    def x_peer(k, c):
        return {"dp": dp, "tensor": lax.rem(x + k, NX) * 2 + c}

    def y_peer(k, c):
        return {"dp": lax.rem(y + k, NY) * NZ + z, "tensor": x * 2 + c}

    def z_peer(k):
        return {"dp": y * NZ + lax.rem(z + k, NZ), "tensor": t}

    z_peers = [{"dp": y * NZ + i + lax.div(i + NZ - z, NZ), "tensor": t} for i in range(NZ - 1)]

    def send(src, dst, ssem, rsem, peer):
        pltpu.make_async_remote_copy(
            src_ref=src, dst_ref=dst, send_sem=ssem, recv_sem=rsem, device_id=peer, device_id_type=MESH
        ).start()

    def arrived(ref, sem):
        pltpu.make_async_remote_copy(
            src_ref=ref, dst_ref=ref, send_sem=send_sem, recv_sem=sem, device_id=x_peer(1, core), device_id_type=MESH
        ).wait_recv()

    def left_here(ref, sem):
        pltpu.make_async_remote_copy(
            src_ref=ref, dst_ref=ref, send_sem=sem, recv_sem=xr.at[0], device_id=x_peer(1, core), device_id_type=MESH
        ).wait_send()

    def signal(sem, peer):
        pl.semaphore_signal(sem, inc=1, device_id=peer, device_id_type=MESH)

    on_core0 = functools.partial(pl.when, core == 0)
    on_core1 = functools.partial(pl.when, core == 1)

    wt_load = pltpu.make_async_copy(wt_hbm, wt, load_sem.at[len(CHUNKS)])
    wt_load.start()

    def load(c):
        rows = pl.ds(*CHUNKS[c][:2])
        for i, hbm in enumerate((g_hbm, e_hbm)):
            pltpu.make_async_copy(hbm.at[:, rows], both.at[i, :, rows], load_sem.at[c]).start()

    load(0)

    barrier = pltpu.get_barrier_semaphore()

    @on_core1()
    def _():
        for k in ORDER4:
            signal(barrier, x_peer(k, 1))
            signal(barrier, x_peer(k, 0))
        for k in (1, NY - 1):
            signal(barrier, y_peer(k, 1))
        for k in (1, NZ - 1):
            signal(barrier, z_peer(k))
        signal(barrier, x_peer(0, 0))

    @on_core0()
    def _():
        for k in ORDER4 + (0,):
            signal(barrier, x_peer(k, 1))

    load(1)

    wt_load.wait()
    load(2)
    load(3)
    w_wide = jnp.concatenate([wt[...] * (1.0 / NY)] * GROUPS, axis=0).T
    group = lax.div(lax.broadcasted_iota(jnp.int32, (COLS, 128), 1), RANK)
    for j in range(GROUPS):
        banded = jnp.where(group == j, w_wide, 0.0)
        wall[COLS * j : COLS * (j + 1), :] = jnp.concatenate(split2(banded), axis=1)
    for c, (first, length, padded) in enumerate(CHUNKS):
        rows = pl.ds(first, length)
        pltpu.make_async_copy(both.at[:, :, rows], both.at[:, :, rows], load_sem.at[c]).wait()
        halves = [
            pad_rows(jnp.concatenate([both[i, j, first : first + length, :] for j in range(GROUPS)], axis=1), padded)
            for i in range(2)
        ]
        acc = jnp.dot(jnp.concatenate(halves, axis=0), wall[...], preferred_element_type=F32)
        acc = acc[:padded] + acc[padded:]
        packed = acc[:, :128] + acc[:, 128:]
        piece = padded // NX
        for i in range(NX):
            part[c, i, :piece] = packed[piece * i : piece * (i + 1)]
        rows = pl.ds(0, piece)
        if c == 0:

            @on_core1()
            def _():
                pl.semaphore_wait(barrier, 2 * (NX - 1) + 1 + 2 + 2)
                for k in (1, NY - 1):
                    signal(reach_y.at[0], y_peer(k, 1))
                for k in (1, NZ - 1):
                    signal(reach_z.at[0], z_peer(k))

            @on_core0()
            def _():
                pl.semaphore_wait(barrier, NX)

        @on_core1()
        def _():
            for k in ORDER4:
                send(part.at[c, lax.rem(x + k, NX), rows], xbuf.at[c, k - 1, rows], send_sem, xr.at[c], x_peer(k, 1))

        @on_core0()
        def _():
            for k in ORDER4 + (0,):
                send(part.at[c, lax.rem(x + k, NX), rows], xbuf.at[c, NX - 1 + k, rows], send_sem, xr.at[c], x_peer(k, 1))

    @on_core1()
    def _():
        pl.semaphore_wait(reach_y.at[0], 2)
        for k in (2, NY - 2):
            signal(reach_y.at[1], y_peer(k, 1))
        for c, (_, _, padded) in enumerate(CHUNKS):
            rows = pl.ds(0, padded // NX)
            arrived(xbuf.at[c, :, rows], xr.at[c])
            if c == 0:
                pl.semaphore_wait(reach_y.at[1], 2)
            total = part[c, x, rows]
            for i in range(2 * NX - 1):
                total = total + xbuf[c, i, rows]
            ybuf[c, y, rows] = total
            for k in ORDER8:
                send(ybuf.at[c, y, rows], ybuf.at[c, y, rows], send_sem, yr.at[c], y_peer(k, 1))
        pl.semaphore_wait(reach_z.at[0], 2)
        for k in (2, NZ - 2):
            signal(reach_z.at[1], z_peer(k))
        for c, (_, _, padded) in enumerate(CHUNKS):
            if c == 1:
                pl.semaphore_wait(reach_z.at[1], 2)
                for k in (2, NZ - 2):
                    signal(reach_z.at[2], z_peer(k))
            rows = pl.ds(0, padded // NX)
            arrived(ybuf.at[c, pl.ds(0, NY - 1), rows], yr.at[c])
            total = ybuf[c, 0, rows]
            for i in range(1, NY):
                total = total + ybuf[c, i, rows]
            pfull[c, x, rows] = total
            for k in ORDER4:
                send(pfull.at[c, x, rows], pfull.at[c, x, rows], send_sem, pr.at[c], x_peer(k, 0))
                send(pfull.at[c, x, rows], pfull.at[c, x, rows], send_sem, pr.at[c], x_peer(k, 1))
            send(pfull.at[c, x, rows], pfull.at[c, x, rows], send_sem, pr.at[c], x_peer(0, 0))

    right = None
    bands = []
    for c, (first, length, padded) in enumerate(CHUNKS):
        rows = pl.ds(0, padded // NX)

        @on_core1()
        def _():
            arrived(pfull.at[c, pl.ds(0, NX - 1), rows], pr.at[c])

        @on_core0()
        def _():
            arrived(pfull.at[c, :, rows], pr.at[c])

        bands.append(jnp.concatenate([pfull[c, i, rows] for i in range(NX)], axis=0)[:length])
        left_t = pad_rows(bands[-1], 128).T
        lt = [left_t[RANK * j : RANK * (j + 1)] for j in range(GROUPS)]
        depth = 128
        if length <= 64:
            depth = 64
            lt = [lt[j] + pltpu.roll(lt[j + 1], 64, 1) for j in range(0, GROUPS, 2)]
        lt = jnp.concatenate(lt, axis=1)
        lhs = jnp.concatenate(split3(lt * (1.0 / NY)), axis=0)
        for i in range(2):
            block = jnp.concatenate(
                [pad_rows(both[i, j, first : first + length, :], depth) for j in range(GROUPS)], axis=0
            )
            term = jnp.dot(lhs, block, preferred_element_type=F32)
            right = term if right is None else right + term
    right = right[:RANK] + (right[RANK : 2 * RANK] + right[2 * RANK :])
    for c in range(RCHUNKS):
        for i in range(NY):
            q, h = i // 2, 2 * (i % 2) + c
            rpart[c, i] = right[8 * q : 8 * q + 8, 128 * h : 128 * (h + 1)]
    left = jnp.concatenate(bands, axis=0)

    @on_core0()
    def _():
        for c in range(RCHUNKS):
            for k in ORDER8 + (0,):
                send(rpart.at[c, lax.rem(y + k, NY)], rbuf.at[c, NY - 1 + k], send_sem, rr.at[c], y_peer(k, 1))
        arrived(gsum, gm)

    @on_core1()
    def _():
        for c in range(RCHUNKS):
            for k in ORDER8:
                send(rpart.at[c, lax.rem(y + k, NY)], rbuf.at[c, k - 1], send_sem, rr.at[c], y_peer(k, 1))

        blocks = jnp.dot(left.T, left, precision=HIGHEST, preferred_element_type=F32)
        lane8 = lax.broadcasted_iota(jnp.int32, (8, 128), 1)
        tile = jnp.zeros((8, 128), F32)
        for q in range(RANK // 8):
            rows8 = None
            for j in range(GROUPS):
                band = blocks[RANK * j + 8 * q : RANK * j + 8 * q + 8, :]
                band = jnp.where(lax.div(lane8, RANK) == j, band, 0.0)
                rows8 = band if rows8 is None else rows8 + band
            rows8 = rows8 + pltpu.roll(rows8, 64, 1)
            rows8 = rows8 + pltpu.roll(rows8, 32, 1)
            tile = jnp.where(lax.div(lane8, RANK) == q, rows8, tile)
        gbuf[z] = tile
        pl.semaphore_wait(reach_z.at[2], 2)
        for peer in z_peers:
            send(gbuf.at[z], gbuf.at[z], send_sem, gr, peer)

        for c in range(RCHUNKS):
            arrived(rbuf.at[c], rr.at[c])
            total = rpart[c, y]
            for i in range(NY - 1):
                total = total + rbuf[c, i]
            zbuf[c, z, 1] = total
            total = rbuf[c, NY - 1]
            for i in range(NY, 2 * NY - 1):
                total = total + rbuf[c, i]
            zbuf[c, z, 0] = total
            for peer in z_peers[:FIRST]:
                send(zbuf.at[c, z], zbuf.at[c, z], send_sem, zr.at[c], peer)
        for peer in z_peers[FIRST:]:
            for c in range(RCHUNKS):
                send(zbuf.at[c, z], zbuf.at[c, z], send_sem, zr.at[c], peer)

        arrived(gbuf.at[pl.ds(0, NZ - 1)], gr)
        tile = gbuf[0]
        for i in range(1, NZ):
            tile = tile + gbuf[i]
        gsum[...] = tile
        send(gsum, gsum, send_sem, gm, x_peer(0, 0))

    tile = gsum[...]
    rows = [tile] + [pltpu.roll(tile, 128 - 32 * q, 1) for q in range(1, RANK // 8)]
    inv = inverse_lower(jnp.concatenate(rows, axis=0))

    @on_core1()
    def _():
        for c in range(RCHUNKS):
            arrived(zbuf.at[c, pl.ds(0, NZ - 1)], zr.at[c])
            total = zbuf[c, 0]
            for i in range(1, NZ):
                total = total + zbuf[c, i]
            zsum[c] = total[0]
            rfull[c, y] = total[1]
            for k in ORDER8:
                send(zsum.at[c], rfull.at[c, y], send_sem, fr.at[c], y_peer(k, 0))
                send(rfull.at[c, y], rfull.at[c, y], send_sem, fr.at[c], y_peer(k, 1))
            send(zsum.at[c], rfull.at[c, y], send_sem, fr.at[c], x_peer(0, 0))

    lane = lax.broadcasted_iota(jnp.int32, (RANK, 128), 1)
    diag = jnp.concatenate(
        [jnp.where(lax.div(lane, RANK) == j, inv, 0.0) for j in range(GROUPS)], axis=0
    )
    left_basis = lax.dot_general(left, diag, (((1,), (1,)), ((), ())), precision=HIGHEST, preferred_element_type=F32)
    b_hi = left_basis.astype(BF16).astype(F32)
    b_lo = left_basis - b_hi
    wide = lax.broadcasted_iota(jnp.int32, (GROUP_ROWS, 128), 1)
    for j in range(GROUPS):
        first = pltpu.roll(b_hi, (128 - RANK * j) % 128, 1) if j else b_hi
        second = pltpu.roll(b_lo, (128 + RANK - RANK * j) % 128, 1) if j != 1 else b_lo
        third = pltpu.roll(b_hi, (128 + 2 * RANK - RANK * j) % 128, 1) if j != 2 else b_hi
        mixed = jnp.where(wide < RANK, first, jnp.where(wide < 2 * RANK, second, third))
        mixed = jnp.where(wide < 3 * RANK, mixed, 0.0)
        lhs_ref[GROUP_ROWS * j : GROUP_ROWS * (j + 1)] = mixed.astype(BF16)
        merged[GROUP_ROWS * j : GROUP_ROWS * (j + 1)] = both[0, j].astype(F32) + both[1, j].astype(F32)
    i_hi, i_mid, i_lo = split3(inv[:, :RANK])
    inv_lhs = jnp.concatenate([i_hi, i_hi, i_mid, i_hi, i_mid, i_lo], axis=1)

    for c in range(RCHUNKS):

        @on_core1()
        def _():
            arrived(rfull.at[c, pl.ds(0, NY - 1)], fr.at[c])

        @on_core0()
        def _():
            arrived(rfull.at[c], fr.at[c])

        rt = jnp.concatenate(
            [jnp.concatenate([rfull[c, 2 * q], rfull[c, 2 * q + 1]], axis=1) for q in range(RANK // 8)], axis=0
        )
        r_hi, r_mid, r_lo = split3(rt)
        basis_t = jnp.dot(
            inv_lhs, jnp.concatenate([r_hi, r_mid, r_hi, r_lo, r_mid, r_hi], axis=0), preferred_element_type=F32
        )
        for h in range(2):
            columns = slice(128 * (2 * h + c), 128 * (2 * h + c + 1))
            nb_ref[:, columns] = basis_t[:, 128 * h : 128 * (h + 1)]

    @on_core0()
    def _():
        left_here(sizes.at[pl.ds(0, SENT0)], send_sem)

    @on_core1()
    def _():
        left_here(sizes, send_sem)


def update_kernel(merged, lhs_ref, basis_ref, err_hbm, nb_hbm, out, sem):
    blocks = ROWS // BLOCK
    stores = [pltpu.make_async_copy(basis_ref, nb_hbm, sem.at[blocks])]
    stores[0].start()
    n_hi, n_lo = split2(basis_ref[...])
    rhs = jnp.concatenate([n_hi, n_hi, n_lo, jnp.zeros_like(n_lo)], axis=0)
    for b in range(blocks):
        sl = slice(BLOCK * b, BLOCK * (b + 1))
        rebuilt = jnp.dot(lhs_ref[sl, :], rhs, preferred_element_type=F32)
        out[sl, :] = (merged[sl, :] - rebuilt).astype(BF16)
        rows = pl.ds(BLOCK * b, BLOCK)
        copy = pltpu.make_async_copy(out.at[rows], err_hbm.at[rows], sem.at[b])
        copy.start()
        stores.append(copy)
    for copy in stores:
        copy.wait()


def on_device(gradients, error_buffer, warm_basis):
    vmem = pl.BlockSpec(memory_space=pltpu.VMEM)
    anyspace = pl.BlockSpec(memory_space=pl.ANY)
    dma = pltpu.SemaphoreType.DMA
    wide = (ROWS, COLS)
    grouped = (GROUPS, GROUP_ROWS, COLS)
    nc, piece = len(CHUNKS), max(padded for _, _, padded in CHUNKS) // NX
    inputs = (gradients.reshape(grouped), error_buffer.reshape(grouped), warm_basis.T)
    kept = pl.pallas_call(
        factors_kernel,
        name="factors",
        out_shape=(
            pltpu.VMEM(wide, F32),
            pltpu.VMEM((ROWS, 128), BF16),
            pltpu.VMEM((RANK, COLS), F32),
        ),
        in_specs=[anyspace, anyspace, anyspace],
        out_specs=(vmem, vmem, vmem),
        scratch_shapes=[
            pltpu.VMEM((2,) + grouped, BF16),
            pltpu.VMEM((RANK, COLS), F32),
            pltpu.VMEM((GROUPS * COLS, 256), BF16),
            pltpu.VMEM((nc, NX, piece, 128), F32),
            pltpu.VMEM((nc, 2 * NX - 1, piece, 128), F32),
            pltpu.VMEM((nc, NY, piece, 128), F32),
            pltpu.VMEM((nc, NX, piece, 128), F32),
            pltpu.VMEM((RCHUNKS, NY, 8, 128), F32),
            pltpu.VMEM((RCHUNKS, 2 * NY - 1, 8, 128), F32),
            pltpu.VMEM((RCHUNKS, NZ, 2, 8, 128), F32),
            pltpu.VMEM((RCHUNKS, 8, 128), F32),
            pltpu.VMEM((NZ, 8, 128), F32),
            pltpu.VMEM((8, 128), F32),
            pltpu.VMEM((RCHUNKS, NY, 8, 128), F32),
            pltpu.VMEM((SENT1, 8, 128), F32),
            dma((nc + 1,)),
            dma,
            dma((nc,)), dma((nc,)), dma((nc,)),
            dma, dma, dma((RCHUNKS,)), dma((RCHUNKS,)), dma((RCHUNKS,)),
            pltpu.SemaphoreType.REGULAR((2,)), pltpu.SemaphoreType.REGULAR((3,)),
        ],
        compiler_params=pltpu.CompilerParams(
            collective_id=0, has_side_effects=True, vmem_limit_bytes=24 * 1024 * 1024
        ),
    )(*(pltpu.with_memory_space_constraint(x, pltpu.HBM) for x in inputs))
    new_errors, basis_t = pl.pallas_call(
        update_kernel,
        name="update",
        out_shape=(jax.ShapeDtypeStruct(wide, BF16), jax.ShapeDtypeStruct((RANK, COLS), F32)),
        in_specs=[vmem, vmem, vmem],
        out_specs=(anyspace, anyspace),
        scratch_shapes=[pltpu.VMEM(wide, BF16), dma((ROWS // BLOCK + 1,))],
        compiler_params=pltpu.CompilerParams(vmem_limit_bytes=24 * 1024 * 1024),
    )(*(pltpu.with_memory_space_constraint(x, pltpu.VMEM) for x in kept))
    return new_errors[None], basis_t.T


def solution(mesh):
    placed = (P("dp", None, "tensor"), P("dp", None, "tensor"), P("tensor", None))
    return jax.shard_map(
        on_device,
        mesh=mesh,
        in_specs=placed,
        out_specs=(P("dp", None, "tensor"), P("tensor", None)),
        check_vma=False,
    )
```

```python
import functools

import jax
import jax.numpy as jnp
from jax import lax
from jax.experimental import pallas as pl
from jax.experimental.pallas import tpu as pltpu
from jax.sharding import PartitionSpec as P

MESH = pl.DeviceIdType.MESH
HIGHEST = lax.Precision.HIGHEST
F32 = jnp.float32
BF16 = jnp.bfloat16

NY = 8
NZ = 12
NX = 4
ROWS = 1344
COLS = 512
RANK = 32
GROUPS = 4
GROUP_ROWS = ROWS // GROUPS
BLOCK = 192
HALF = COLS // 2
CHUNKS = ((0, 96, 96), (96, 128, 128), (224, 112, 128))
PACKED = sum(padded for _, _, padded in CHUNKS)
RCHUNKS = 2

SENT0 = NX * PACKED // NX // 8 + RCHUNKS * NY
SENT1 = (17 * PACKED // NX // 8) + RCHUNKS * 7 + 11 + RCHUNKS * 11 * 2 + 1 + RCHUNKS * 15
FIRST = 1
ORDER4 = (2, 1, 3)
ORDER8 = (4, 3, 5, 2, 6, 1, 7)


def pad_rows(block, rows):
    if block.shape[0] == rows:
        return block
    return jnp.concatenate([block, jnp.zeros((rows - block.shape[0], block.shape[1]), block.dtype)], axis=0)


def split2(x):
    hi = x.astype(BF16)
    return hi, (x - hi.astype(F32)).astype(BF16)


def split3(x):
    hi = x.astype(BF16)
    rest = x - hi.astype(F32)
    mid = rest.astype(BF16)
    return hi, mid, (rest - mid.astype(F32)).astype(BF16)


def inverse_lower(gram):
    lane = lax.broadcasted_iota(jnp.int32, (RANK, 128), 1)
    row = lax.broadcasted_iota(jnp.int32, (RANK, 128), 0)
    a = jnp.where(lane < RANK, gram, jnp.where(lane == row + RANK, 1.0, 0.0))
    for k in range(RANK - 1):
        pivot = a[k : k + 1, :]
        factor = a[:, k : k + 1] * (1.0 / pivot[:, k : k + 1])
        factor = jnp.where(row[:, :1] > k, factor, 0.0)
        a = a - factor * pivot
    diagonal = jnp.sum(jnp.where(lane == row, a, 0.0), axis=1, keepdims=True)
    inv = a * lax.rsqrt(diagonal)
    inv = jnp.where((lane >= RANK) & (lane < 2 * RANK), inv, 0.0)
    inv = inv + pltpu.roll(inv, 2 * RANK, 1)
    return inv + pltpu.roll(inv, RANK, 1)


def update_rhs(basis_t):
    hi, lo = split2(basis_t)
    return jnp.concatenate([hi, hi, lo, jnp.zeros_like(lo)], axis=0)


def factors_kernel(
    g_hbm, e_hbm, wt_hbm, merged, lhs_ref, nb_ref, done,
    both, wt, wall, part, xbuf, ybuf, pfull, rpart, rbuf, zbuf, zsum, gbuf, gsum, rfull, sizes,
    load_sem, send_sem, xr, yr, pr, gr, gm, rr, zr, fr, reach_y, reach_z,
):
    dp = lax.axis_index("dp")
    t = lax.axis_index("tensor")
    y = lax.div(dp, NZ)
    z = lax.rem(dp, NZ)
    x = lax.div(t, 2)
    core = lax.rem(t, 2)

    def x_peer(k, c):
        return {"dp": dp, "tensor": lax.rem(x + k, NX) * 2 + c}

    def y_peer(k, c):
        return {"dp": lax.rem(y + k, NY) * NZ + z, "tensor": x * 2 + c}

    def z_peer(k):
        return {"dp": y * NZ + lax.rem(z + k, NZ), "tensor": t}

    z_peers = [{"dp": y * NZ + i + lax.div(i + NZ - z, NZ), "tensor": t} for i in range(NZ - 1)]

    y_rows = [(i + lax.div(i + NY - y, NY)) * NZ + z for i in range(NY - 1)]
    y_peers = [[{"dp": row, "tensor": x * 2 + c} for c in range(2)] for row in y_rows]

    def send(src, dst, ssem, rsem, peer):
        pltpu.make_async_remote_copy(
            src_ref=src, dst_ref=dst, send_sem=ssem, recv_sem=rsem, device_id=peer, device_id_type=MESH
        ).start()

    def arrived(ref, sem):
        pltpu.make_async_remote_copy(
            src_ref=ref, dst_ref=ref, send_sem=send_sem, recv_sem=sem, device_id=x_peer(1, core), device_id_type=MESH
        ).wait_recv()

    def left_here(ref, sem):
        pltpu.make_async_remote_copy(
            src_ref=ref, dst_ref=ref, send_sem=sem, recv_sem=xr.at[0], device_id=x_peer(1, core), device_id_type=MESH
        ).wait_send()

    def signal(sem, peer):
        pl.semaphore_signal(sem, inc=1, device_id=peer, device_id_type=MESH)

    on_core0 = functools.partial(pl.when, core == 0)
    on_core1 = functools.partial(pl.when, core == 1)

    wt_load = pltpu.make_async_copy(wt_hbm, wt, load_sem.at[len(CHUNKS)])
    wt_load.start()

    def load(c):
        rows = pl.ds(*CHUNKS[c][:2])
        for i, hbm in enumerate((g_hbm, e_hbm)):
            pltpu.make_async_copy(hbm.at[:, rows], both.at[i, :, rows], load_sem.at[c]).start()

    load(0)

    barrier = pltpu.get_barrier_semaphore()

    @on_core1()
    def _():
        for k in ORDER4:
            signal(barrier, x_peer(k, 1))
            signal(barrier, x_peer(k, 0))
        for k in (1, NY - 1):
            signal(barrier, y_peer(k, 1))
        for k in (1, NZ - 1):
            signal(barrier, z_peer(k))
        signal(barrier, x_peer(0, 0))

    @on_core0()
    def _():
        for k in ORDER4 + (0,):
            signal(barrier, x_peer(k, 1))

    load(1)

    wt_load.wait()
    load(2)
    w_wide = jnp.concatenate([wt[...] * (1.0 / NY)] * GROUPS, axis=0).T
    group = lax.div(lax.broadcasted_iota(jnp.int32, (COLS, 128), 1), RANK)
    for j in range(GROUPS):
        banded = jnp.where(group == j, w_wide, 0.0)
        wall[COLS * j : COLS * (j + 1), :] = jnp.concatenate(split2(banded), axis=1)
    for c, (first, length, padded) in enumerate(CHUNKS):
        rows = pl.ds(first, length)
        pltpu.make_async_copy(both.at[:, :, rows], both.at[:, :, rows], load_sem.at[c]).wait()
        halves = [
            pad_rows(jnp.concatenate([both[i, j, first : first + length, :] for j in range(GROUPS)], axis=1), padded)
            for i in range(2)
        ]
        acc = jnp.dot(jnp.concatenate(halves, axis=0), wall[...], preferred_element_type=F32)
        acc = acc[:padded] + acc[padded:]
        packed = acc[:, :128] + acc[:, 128:]
        piece = padded // NX
        for i in range(NX):
            part[c, i, :piece] = packed[piece * i : piece * (i + 1)]
        rows = pl.ds(0, piece)
        if c == 0:

            @on_core1()
            def _():
                pl.semaphore_wait(barrier, 2 * (NX - 1) + 1 + 2 + 2)
                for k in (1, NY - 1):
                    signal(reach_y.at[0], y_peer(k, 1))
                for k in (1, NZ - 1):
                    signal(reach_z.at[0], z_peer(k))

            @on_core0()
            def _():
                pl.semaphore_wait(barrier, NX)

        @on_core1()
        def _():
            for k in ORDER4:
                send(part.at[c, lax.rem(x + k, NX), rows], xbuf.at[c, k - 1, rows], send_sem, xr.at[c], x_peer(k, 1))

        @on_core0()
        def _():
            for k in ORDER4 + (0,):
                send(part.at[c, lax.rem(x + k, NX), rows], xbuf.at[c, NX - 1 + k, rows], send_sem, xr.at[c], x_peer(k, 1))

    @on_core1()
    def _():
        pl.semaphore_wait(reach_y.at[0], 2)
        for k in (2, NY - 2):
            signal(reach_y.at[1], y_peer(k, 1))
        for c, (_, _, padded) in enumerate(CHUNKS):
            rows = pl.ds(0, padded // NX)
            arrived(xbuf.at[c, :, rows], xr.at[c])
            if c == 0:
                pl.semaphore_wait(reach_y.at[1], 2)
            total = part[c, x, rows]
            for i in range(2 * NX - 1):
                total = total + xbuf[c, i, rows]
            ybuf[c, y, rows] = total
            for k in ORDER8:
                send(ybuf.at[c, y, rows], ybuf.at[c, y, rows], send_sem, yr.at[c], y_peer(k, 1))
        pl.semaphore_wait(reach_z.at[0], 2)
        for k in (2, NZ - 2):
            signal(reach_z.at[1], z_peer(k))
        for c, (_, _, padded) in enumerate(CHUNKS):
            if c == 1:
                pl.semaphore_wait(reach_z.at[1], 2)
                for k in (2, NZ - 2):
                    signal(reach_z.at[2], z_peer(k))
            rows = pl.ds(0, padded // NX)
            arrived(ybuf.at[c, pl.ds(0, NY - 1), rows], yr.at[c])
            total = ybuf[c, 0, rows]
            for i in range(1, NY):
                total = total + ybuf[c, i, rows]
            pfull[c, x, rows] = total
            for k in ORDER4:
                send(pfull.at[c, x, rows], pfull.at[c, x, rows], send_sem, pr.at[c], x_peer(k, 0))
                send(pfull.at[c, x, rows], pfull.at[c, x, rows], send_sem, pr.at[c], x_peer(k, 1))
            send(pfull.at[c, x, rows], pfull.at[c, x, rows], send_sem, pr.at[c], x_peer(0, 0))

    right = None
    bands = []
    for c, (first, length, padded) in enumerate(CHUNKS):
        rows = pl.ds(0, padded // NX)

        @on_core1()
        def _():
            arrived(pfull.at[c, pl.ds(0, NX - 1), rows], pr.at[c])

        @on_core0()
        def _():
            arrived(pfull.at[c, :, rows], pr.at[c])

        bands.append(jnp.concatenate([pfull[c, i, rows] for i in range(NX)], axis=0)[:length])
        left_t = pad_rows(bands[-1], 128).T
        lt = [left_t[RANK * j : RANK * (j + 1)] for j in range(GROUPS)]
        depth = 128
        if length <= 64:
            depth = 64
            lt = [lt[j] + pltpu.roll(lt[j + 1], 64, 1) for j in range(0, GROUPS, 2)]
        lt = jnp.concatenate(lt, axis=1)
        lhs = jnp.concatenate(split3(lt * (1.0 / NY)), axis=0)
        for i in range(2):
            block = jnp.concatenate(
                [pad_rows(both[i, j, first : first + length, :], depth) for j in range(GROUPS)], axis=0
            )
            term = jnp.dot(lhs, block, preferred_element_type=F32)
            right = term if right is None else right + term
    right = right[:RANK] + (right[RANK : 2 * RANK] + right[2 * RANK :])
    for c in range(RCHUNKS):
        for i in range(NY):
            q, h = i // 2, 2 * c + i % 2
            rpart[c, i] = right[8 * q : 8 * q + 8, 128 * h : 128 * (h + 1)]
    left = jnp.concatenate(bands, axis=0)

    @on_core0()
    def _():
        for c in range(RCHUNKS):
            for k in ORDER8 + (0,):
                send(rpart.at[c, lax.rem(y + k, NY)], rbuf.at[c, NY - 1 + k], send_sem, rr.at[c], y_peer(k, 1))
        arrived(gsum, gm)

    @on_core1()
    def _():
        for c in range(RCHUNKS):
            for k in ORDER8:
                send(rpart.at[c, lax.rem(y + k, NY)], rbuf.at[c, k - 1], send_sem, rr.at[c], y_peer(k, 1))

        blocks = jnp.dot(left.T, left, precision=HIGHEST, preferred_element_type=F32)
        lane8 = lax.broadcasted_iota(jnp.int32, (8, 128), 1)
        tile = jnp.zeros((8, 128), F32)
        for q in range(RANK // 8):
            rows8 = None
            for j in range(GROUPS):
                band = blocks[RANK * j + 8 * q : RANK * j + 8 * q + 8, :]
                band = jnp.where(lax.div(lane8, RANK) == j, band, 0.0)
                rows8 = band if rows8 is None else rows8 + band
            rows8 = rows8 + pltpu.roll(rows8, 64, 1)
            rows8 = rows8 + pltpu.roll(rows8, 32, 1)
            tile = jnp.where(lax.div(lane8, RANK) == q, rows8, tile)
        gbuf[z] = tile
        pl.semaphore_wait(reach_z.at[2], 2)
        for peer in z_peers:
            send(gbuf.at[z], gbuf.at[z], send_sem, gr, peer)

        for c in range(RCHUNKS):
            arrived(rbuf.at[c], rr.at[c])
            total = rpart[c, y]
            for i in range(NY - 1):
                total = total + rbuf[c, i]
            zbuf[c, z, 1] = total
            total = rbuf[c, NY - 1]
            for i in range(NY, 2 * NY - 1):
                total = total + rbuf[c, i]
            zbuf[c, z, 0] = total
            for peer in z_peers[:FIRST]:
                send(zbuf.at[c, z], zbuf.at[c, z], send_sem, zr.at[c], peer)
        for peer in z_peers[FIRST:]:
            for c in range(RCHUNKS):
                send(zbuf.at[c, z], zbuf.at[c, z], send_sem, zr.at[c], peer)

        arrived(gbuf.at[pl.ds(0, NZ - 1)], gr)
        tile = gbuf[0]
        for i in range(1, NZ):
            tile = tile + gbuf[i]
        gsum[...] = tile
        send(gsum, gsum, send_sem, gm, x_peer(0, 0))

    tile = gsum[...]
    rows = [tile] + [pltpu.roll(tile, 128 - 32 * q, 1) for q in range(1, RANK // 8)]
    inv = inverse_lower(jnp.concatenate(rows, axis=0))

    @on_core1()
    def _():
        for c in range(RCHUNKS):
            arrived(zbuf.at[c, pl.ds(0, NZ - 1)], zr.at[c])
            total = zbuf[c, 0]
            for i in range(1, NZ):
                total = total + zbuf[c, i]
            zsum[c] = total[0]
            rfull[c, y] = total[1]
            for peer0, peer1 in y_peers:
                send(rfull.at[c, y], rfull.at[c, y], send_sem, fr.at[c], peer1)
                send(zsum.at[c], rfull.at[c, y], send_sem, fr.at[c], peer0)
            send(zsum.at[c], rfull.at[c, y], send_sem, fr.at[c], x_peer(0, 0))

    lane = lax.broadcasted_iota(jnp.int32, (RANK, 128), 1)
    diag = jnp.concatenate(
        [jnp.where(lax.div(lane, RANK) == j, inv, 0.0) for j in range(GROUPS)], axis=0
    )
    left_basis = lax.dot_general(left, diag, (((1,), (1,)), ((), ())), precision=HIGHEST, preferred_element_type=F32)
    b_hi = left_basis.astype(BF16).astype(F32)
    b_lo = left_basis - b_hi
    wide = lax.broadcasted_iota(jnp.int32, (GROUP_ROWS, 128), 1)
    for j in range(GROUPS):
        first = pltpu.roll(b_hi, (128 - RANK * j) % 128, 1) if j else b_hi
        second = pltpu.roll(b_lo, (128 + RANK - RANK * j) % 128, 1) if j != 1 else b_lo
        third = pltpu.roll(b_hi, (128 + 2 * RANK - RANK * j) % 128, 1) if j != 2 else b_hi
        mixed = jnp.where(wide < RANK, first, jnp.where(wide < 2 * RANK, second, third))
        mixed = jnp.where(wide < 3 * RANK, mixed, 0.0)
        lhs_ref[GROUP_ROWS * j : GROUP_ROWS * (j + 1)] = mixed.astype(BF16)
        merged[GROUP_ROWS * j : GROUP_ROWS * (j + 1)] = both[0, j].astype(F32) + both[1, j].astype(F32)
    i_hi, i_mid, i_lo = split3(inv[:, :RANK])
    inv_lhs = jnp.concatenate([i_hi, i_hi, i_mid, i_hi, i_mid, i_lo], axis=1)

    for c in range(RCHUNKS):

        @on_core1()
        def _():
            arrived(rfull.at[c, pl.ds(0, NY - 1)], fr.at[c])

        @on_core0()
        def _():
            arrived(rfull.at[c], fr.at[c])

        rt = jnp.concatenate(
            [jnp.concatenate([rfull[c, 2 * q], rfull[c, 2 * q + 1]], axis=1) for q in range(RANK // 8)], axis=0
        )
        r_hi, r_mid, r_lo = split3(rt)
        basis_t = jnp.dot(
            inv_lhs, jnp.concatenate([r_hi, r_mid, r_hi, r_lo, r_mid, r_hi], axis=0), preferred_element_type=F32
        )
        nb_ref[:, HALF * c : HALF * (c + 1)] = basis_t
        if c == 0:
            rhs = update_rhs(basis_t)
            for b in range(ROWS // BLOCK):
                rows = slice(BLOCK * b, BLOCK * (b + 1))
                rebuilt = jnp.dot(lhs_ref[rows, :], rhs, preferred_element_type=F32)
                done[rows, :] = (merged[rows, :HALF] - rebuilt).astype(BF16)

    @on_core0()
    def _():
        left_here(sizes.at[pl.ds(0, SENT0)], send_sem)

    @on_core1()
    def _():
        left_here(sizes, send_sem)


def update_kernel(merged, lhs_ref, basis_ref, done, err_hbm, nb_hbm, out, sem):
    blocks = ROWS // BLOCK
    stores = [
        pltpu.make_async_copy(done, err_hbm.at[:, pl.ds(0, HALF)], sem.at[blocks]),
        pltpu.make_async_copy(basis_ref, nb_hbm, sem.at[blocks + 1]),
    ]
    for copy in stores:
        copy.start()
    rhs = update_rhs(basis_ref[:, HALF:])
    for b in range(blocks):
        sl = slice(BLOCK * b, BLOCK * (b + 1))
        rebuilt = jnp.dot(lhs_ref[sl, :], rhs, preferred_element_type=F32)
        out[sl, :] = (merged[sl, HALF:] - rebuilt).astype(BF16)
        rows = pl.ds(BLOCK * b, BLOCK)
        copy = pltpu.make_async_copy(out.at[rows], err_hbm.at[rows, pl.ds(HALF, HALF)], sem.at[b])
        copy.start()
        stores.append(copy)
    for copy in stores:
        copy.wait()


def on_device(gradients, error_buffer, warm_basis):
    vmem = pl.BlockSpec(memory_space=pltpu.VMEM)
    anyspace = pl.BlockSpec(memory_space=pl.ANY)
    dma = pltpu.SemaphoreType.DMA
    wide = (ROWS, COLS)
    grouped = (GROUPS, GROUP_ROWS, COLS)
    nc, piece = len(CHUNKS), max(padded for _, _, padded in CHUNKS) // NX
    inputs = (gradients.reshape(grouped), error_buffer.reshape(grouped), warm_basis.T)
    kept = pl.pallas_call(
        factors_kernel,
        name="factors",
        out_shape=(
            pltpu.VMEM(wide, F32),
            pltpu.VMEM((ROWS, 128), BF16),
            pltpu.VMEM((RANK, COLS), F32),
            pltpu.VMEM((ROWS, HALF), BF16),
        ),
        in_specs=[anyspace, anyspace, anyspace],
        out_specs=(vmem, vmem, vmem, vmem),
        scratch_shapes=[
            pltpu.VMEM((2,) + grouped, BF16),
            pltpu.VMEM((RANK, COLS), F32),
            pltpu.VMEM((GROUPS * COLS, 256), BF16),
            pltpu.VMEM((nc, NX, piece, 128), F32),
            pltpu.VMEM((nc, 2 * NX - 1, piece, 128), F32),
            pltpu.VMEM((nc, NY, piece, 128), F32),
            pltpu.VMEM((nc, NX, piece, 128), F32),
            pltpu.VMEM((RCHUNKS, NY, 8, 128), F32),
            pltpu.VMEM((RCHUNKS, 2 * NY - 1, 8, 128), F32),
            pltpu.VMEM((RCHUNKS, NZ, 2, 8, 128), F32),
            pltpu.VMEM((RCHUNKS, 8, 128), F32),
            pltpu.VMEM((NZ, 8, 128), F32),
            pltpu.VMEM((8, 128), F32),
            pltpu.VMEM((RCHUNKS, NY, 8, 128), F32),
            pltpu.VMEM((SENT1, 8, 128), F32),
            dma((nc + 1,)),
            dma,
            dma((nc,)), dma((nc,)), dma((nc,)),
            dma, dma, dma((RCHUNKS,)), dma((RCHUNKS,)), dma((RCHUNKS,)),
            pltpu.SemaphoreType.REGULAR((2,)), pltpu.SemaphoreType.REGULAR((3,)),
        ],
        compiler_params=pltpu.CompilerParams(
            collective_id=0, has_side_effects=True, vmem_limit_bytes=24 * 1024 * 1024
        ),
    )(*(pltpu.with_memory_space_constraint(x, pltpu.HBM) for x in inputs))
    new_errors, basis_t = pl.pallas_call(
        update_kernel,
        name="update",
        out_shape=(jax.ShapeDtypeStruct(wide, BF16), jax.ShapeDtypeStruct((RANK, COLS), F32)),
        in_specs=[vmem, vmem, vmem, vmem],
        out_specs=(anyspace, anyspace),
        scratch_shapes=[pltpu.VMEM((ROWS, HALF), BF16), dma((ROWS // BLOCK + 2,))],
        compiler_params=pltpu.CompilerParams(vmem_limit_bytes=24 * 1024 * 1024),
    )(*(pltpu.with_memory_space_constraint(x, pltpu.VMEM) for x in kept))
    return new_errors[None], basis_t.T


def solution(mesh):
    placed = (P("dp", None, "tensor"), P("dp", None, "tensor"), P("tensor", None))
    return jax.shard_map(
        on_device,
        mesh=mesh,
        in_specs=placed,
        out_specs=(P("dp", None, "tensor"), P("tensor", None)),
        check_vma=False,
    )
```
